256 devices in a mesh: section: 8 (over x, core), patch: 32 (over y, z).
Axes of the slice: x: 4, y: 4, z: 8, core: 2. Of those that a mesh axis runs over, the one named last changes fastest.
Arguments:
- arriving: bfloat16 [8, 32, 384, 1536], P('section', 'patch'), may hold values from -6 to 6
- modulation: float32 [8, 2, 1536], P('section'), may hold values from -3 to 3
- gate: float32 [8, 1536], P('section'), may hold values from 1 to 4
- w_query: bfloat16 [8, 1536, 1536], P('section', 'patch'), may hold values from -0.15625 to 0.15625
- w_kv: bfloat16 [8, 1536, 3072], P('section'), may hold values from -0.15625 to 0.15625
- w_out: bfloat16 [8, 1536, 1536], P('section', 'patch'), may hold values from -0.15625 to 0.15625
- qk_gain: float32 [8, 2, 1536], P('section'), may hold values from 0.56 to 6
- neighbors: int32 [32, 4], P('patch'), may hold values from 0 to 31, as said below
- live: int32 [32], P('patch'), may hold values from 2 to 4, as said below
Outputs:
- handed: bfloat16 [8, 32, 384, 1536], P('section', 'patch')
The draws below stay inside these ranges and needn't reach their ends.
Inputs may be any that keep to these rules, and one draw needn't show every extreme that they name: `neighbors`: row i names tile i in slot 0 and, in slots 1 to live[i] - 1, distinct other tiles j with |i - j| <= 2; slots from live[i] on name i. `live`: some tile uses all 4 slots.
All inputs are finite; a program needn't handle non-finite values.
Results may differ from the reference program's by a relative error of at most 0.0065.
The reference program's roundings to bfloat16 on the way count: a program that leaves them out, or rounds other values in their place, can miss the bound.
Values may be sent and summed in bfloat16 or wider, within the bound.
No kernel may reach another device: no remote copies, remote signals or barrier semaphores. Data moves between devices by JAX's collectives and lax.ppermute only.
A program may use at most 128 MiB of HBM per device.

```python
import math
import jax
import jax.numpy as jnp
from jax import lax

D = 1536
HEADS = 12
HEAD_DIM = 128
INNER = 1536
TILE = 384
SPAN = 2
NB = 4
TILES = 32
N_SECTION = 8


def tile_lists(key):
    base_key = jax.random.fold_in(key, 17)
    order_key, count_key = jax.random.split(base_key)
    position = jnp.arange(TILES, dtype=jnp.int32)
    offsets = jnp.concatenate([jnp.arange(-SPAN, 0, dtype=jnp.int32), jnp.arange(1, SPAN + 1, dtype=jnp.int32)])
    candidate = position[:, None] + offsets[None, :]
    usable = (candidate >= 0) & (candidate < TILES)
    column = jnp.arange(2 * SPAN, dtype=jnp.int32)
    ranking = jax.random.randint(order_key, (TILES, 2 * SPAN), 0, 1000, dtype=jnp.int32) * (2 * SPAN) + column[None, :]
    ranking = jnp.where(usable, ranking, 1000000 + column[None, :])
    ordering = jnp.argsort(ranking, axis=1)
    picked = jnp.take_along_axis(candidate, ordering, axis=1)[:, :NB - 1]
    usable_count = jnp.sum(usable.astype(jnp.int32), axis=1)
    wanted = jax.random.randint(count_key, (TILES,), 2, NB + 1, dtype=jnp.int32)
    wanted = jnp.where(position == TILES // 2, NB, wanted)
    counts = jnp.minimum(wanted, usable_count + 1)
    slots = jnp.concatenate([position[:, None], picked], axis=1)
    slot_live = jnp.arange(NB, dtype=jnp.int32)[None, :] < counts[:, None]
    slots = jnp.where(slot_live, slots, position[:, None])
    return (slots.astype(jnp.int32), counts.astype(jnp.int32))


def draw_neighbors(key, part):
    return tile_lists(key)[0]


def draw_live(key, part):
    return tile_lists(key)[1]


def draw_qk_gain(key, part):
    head_key, channel_key = jax.random.split(jax.random.fold_in(key, 5))
    lower_end = 0.7
    upper_end = 3.0
    head_scale = jnp.exp(jax.random.uniform(head_key, (N_SECTION, 2, HEADS, 1), jnp.float32, math.log(lower_end), math.log(upper_end)))
    jitter = jax.random.uniform(channel_key, (N_SECTION, 2, HEADS, HEAD_DIM), jnp.float32, 0.8, 1.2)
    return (head_scale * jitter).reshape(N_SECTION, 2, HEADS * HEAD_DIM)


def shard_levels(key, shape, cuts, low, largest):
    gain, own = 1.0, jax.random.fold_in(key, 6)
    for axis_at, shards_of in cuts:
        steps = jnp.exp(jax.random.uniform(jax.random.fold_in(own, axis_at), (shards_of,), jnp.float32, low / len(cuts), largest / len(cuts)))
        gain = gain * jnp.repeat(steps, shape[axis_at] // shards_of).reshape([-1 if axis == axis_at else 1 for axis in range(len(shape))])
    return gain


def bell_draw(stream_key, extent, spread, reach, pieces=(), kind=jnp.bfloat16):
    loudness = shard_levels(stream_key, extent, pieces, -0.22, 0.18) if pieces else 1.0
    result = jax.random.normal(stream_key, extent, jnp.float32) * spread * loudness
    return jnp.minimum(jnp.maximum(result, -reach), reach).astype(kind)


def setup_inputs(seed: int = 0) -> dict:
    key_list = jax.random.split(jax.random.key(seed), 10)
    arriving = bell_draw(key_list[0], (N_SECTION, TILES, TILE, D), 1.0, 6.0, ((0, 8), (1, 32)))
    modulation = bell_draw(key_list[1], (N_SECTION, 2, D), 0.5, 3.0, ((0, 8),), jnp.float32)
    gate = jnp.clip(jnp.exp(math.log(4.0) - 1.3862944 * jax.random.uniform(key_list[2], (N_SECTION, D), jnp.float32) ** shard_levels(key_list[2], (N_SECTION, D), ((0, 8),), -0.2, 0.2)), 1.0, 4.0)
    w_query = bell_draw(key_list[3], (N_SECTION, D, INNER), D ** -0.5, 0.15625, ((0, 8), (1, 32)))
    w_kv = bell_draw(key_list[4], (N_SECTION, D, 2 * INNER), D ** -0.5, 0.15625, ((0, 8),))
    w_out = bell_draw(key_list[5], (N_SECTION, INNER, D), INNER ** -0.5, 0.15625, ((0, 8), (1, 32)))
    qk_gain = draw_qk_gain(jax.random.fold_in(key_list[9], 71), 0)
    neighbors = draw_neighbors(jax.random.fold_in(key_list[9], 71), 0)
    live = draw_live(jax.random.fold_in(key_list[9], 71), 0)
    return dict(arriving=arriving, modulation=modulation, gate=gate, w_query=w_query, w_kv=w_kv, w_out=w_out, qk_gain=qk_gain, neighbors=neighbors, live=live)


def layer_norm(values):
    average = lax.optimization_barrier(jnp.mean(values, axis=-1, keepdims=True))
    centered = values - average
    variance = lax.optimization_barrier(jnp.mean(centered * centered, axis=-1, keepdims=True))
    return centered * lax.rsqrt(variance + 1e-06)

def head_norm(values, gains):
    count_rows = values.shape[0]
    shaped = values.reshape(count_rows, HEADS, HEAD_DIM)
    square = lax.optimization_barrier(jnp.mean(shaped * shaped, axis=-1, keepdims=True))
    normed = (shaped * lax.rsqrt(square + 1e-06)).reshape(count_rows, INNER)
    return (normed * gains).astype(jnp.bfloat16)

def one_section(arriving, modulation, gate, w_query, w_kv, w_out, qk_gain, neighbors, live):
    residual = arriving.reshape(TILES * TILE, D).astype(jnp.float32)
    normed = (layer_norm(residual) * (1.0 + modulation[1]) + modulation[0]).astype(jnp.bfloat16)
    raw_query = jnp.dot(normed, w_query, preferred_element_type=jnp.float32)
    raw_kv = jnp.dot(normed, w_kv, preferred_element_type=jnp.float32)
    query = head_norm(raw_query, qk_gain[0]).reshape(TILES, TILE, HEADS, HEAD_DIM)
    keys = head_norm(raw_kv[:, :INNER], qk_gain[1]).reshape(TILES, TILE, HEADS, HEAD_DIM)
    values = raw_kv[:, INNER:].astype(jnp.bfloat16).reshape(TILES, TILE, HEADS, HEAD_DIM)
    scale = 1.0 / math.sqrt(HEAD_DIM)

    def per_tile(inputs):
        tile_query, slots, count = inputs
        tile_keys = jnp.take(keys, slots, axis=0).reshape(NB * TILE, HEADS, HEAD_DIM)
        tile_values = jnp.take(values, slots, axis=0).reshape(NB * TILE, HEADS, HEAD_DIM)
        scores = jnp.einsum('qhd,khd->hqk', tile_query.astype(jnp.float32), tile_keys.astype(jnp.float32)) * scale
        key_live = jnp.arange(NB * TILE, dtype=jnp.int32) // TILE < count
        scores = jnp.where(key_live[None, None, :], scores, -1e+30)
        highest = lax.optimization_barrier(jnp.max(scores, axis=-1, keepdims=True))
        exponent = jnp.exp(scores - highest)
        total = lax.optimization_barrier(jnp.sum(exponent, axis=-1, keepdims=True))
        prob_bf = (exponent / total).astype(jnp.bfloat16)
        mixed = jnp.einsum('hqk,khd->qhd', prob_bf.astype(jnp.float32), tile_values.astype(jnp.float32))
        return mixed.astype(jnp.bfloat16).reshape(TILE, INNER)
    attended = lax.map(per_tile, (query, neighbors, live)).reshape(TILES * TILE, INNER)
    branch = jnp.dot(attended, w_out, preferred_element_type=jnp.float32)
    return (residual + gate * branch).astype(jnp.bfloat16).reshape(TILES, TILE, D)

def reference(arriving, modulation, gate, w_query, w_kv, w_out, qk_gain, neighbors, live):

    def section_fn(inputs):
        return one_section(inputs[0], inputs[1], inputs[2], inputs[3], inputs[4], inputs[5], inputs[6], neighbors, live)
    outputs = lax.map(section_fn, (arriving, modulation, gate, w_query, w_kv, w_out, qk_gain))
    return jnp.roll(outputs, 1, axis=0)
```

```python
import math

import jax
import jax.numpy as jnp
from jax import lax
from jax.experimental import pallas as pl
from jax.experimental.pallas import tpu as pltpu
from jax.sharding import PartitionSpec as P

HEADS = 12
HEAD_DIM = 128
SPAN = 2
NB = 4
Y, Z = 4, 8
KV_COLS = 512
HEAD_GROUP = 2
LIMIT = 56 * 1024 * 1024


def shifted(value, steps):
    count = Y * Z
    return lax.ppermute(
        value, "patch", [(i, i + steps) for i in range(count) if 0 <= i + steps < count]
    )


def along_z(value, steps):
    return lax.ppermute(
        value, "patch", [(y * Z + z, y * Z + (z + steps) % Z) for y in range(Y) for z in range(Z)]
    )


def along_y(value, steps):
    return lax.ppermute(
        value, "patch", [(y * Z + z, ((y + steps) % Y) * Z + z) for y in range(Y) for z in range(Z)]
    )


def to_next_section(block):
    count = lax.axis_size("section")
    return lax.ppermute(block, "section", [(i, (i + 1) % count) for i in range(count)])


def norm_rows(x_ref, modulation_ref):
    values = x_ref[...].astype(jnp.float32)
    width = values.shape[1]
    average = jnp.sum(values, axis=-1, keepdims=True) * (1.0 / width)
    centered = values - average
    variance = jnp.sum(centered * centered, axis=-1, keepdims=True) * (1.0 / width)
    scaled = centered * lax.rsqrt(variance + 1e-06)
    return (scaled * (1.0 + modulation_ref[1:2]) + modulation_ref[0:1]).astype(jnp.bfloat16)


def head_norm(raw, gains):
    parts = []
    for h in range(raw.shape[1] // HEAD_DIM):
        piece = raw[:, h * HEAD_DIM : (h + 1) * HEAD_DIM]
        square = jnp.sum(piece * piece, axis=-1, keepdims=True) * (1.0 / HEAD_DIM)
        gain = gains[:, h * HEAD_DIM : (h + 1) * HEAD_DIM]
        parts.append((piece * lax.rsqrt(square + 1e-06) * gain).astype(jnp.bfloat16))
    return jnp.concatenate(parts, axis=1) if len(parts) > 1 else parts[0]


def kv_tiles(tiles, modulation, w_kv, gains, start, window):
    count = len(tiles)
    rows, width = tiles[0].shape
    wide = w_kv.shape[1]
    inner = wide // 2
    steps = wide // KV_COLS
    half = steps // 2
    first = window is None

    def body(*refs):
        x_refs = refs[:count]
        modulation_ref, w_ref, gain_ref = refs[count : count + 3]
        rest = refs[count + 3 :]
        if not first:
            rest = rest[1:]
        if first:
            kv_ref, normed_out, normed = rest
        else:
            kv_ref, normed = rest
        step = pl.program_id(0)

        @pl.when(step == 0)
        def _():
            for i in range(count):
                normed[i * rows : (i + 1) * rows, :] = norm_rows(x_refs[i], modulation_ref)
            if first:
                normed_out[...] = normed[...]

        for i in range(count):
            raw = jnp.dot(
                normed[i * rows : (i + 1) * rows, :], w_ref[...], preferred_element_type=jnp.float32
            )

            @pl.when(step < half)
            def _():
                kv_ref[i] = head_norm(raw, gain_ref[...])

            @pl.when(step >= half)
            def _():
                kv_ref[i] = raw.astype(jnp.bfloat16)

    in_specs = [pl.BlockSpec((rows, width), lambda j: (0, 0)) for _ in tiles]
    in_specs += [
        pl.BlockSpec((2, width), lambda j: (0, 0)),
        pl.BlockSpec((width, KV_COLS), lambda j: (0, j)),
        pl.BlockSpec((1, KV_COLS), lambda j: (0, jnp.minimum(j, half - 1))),
    ]
    operands = list(tiles) + [modulation, w_kv, gains]
    aliases = {}
    shapes = [jax.ShapeDtypeStruct((2 * SPAN + 1, rows, wide), jnp.bfloat16)]
    block_at = start // count
    out_specs = [pl.BlockSpec((count, rows, KV_COLS), lambda j: (block_at, 0, j))]
    if first:
        shapes.append(jax.ShapeDtypeStruct((rows, width), jnp.bfloat16))
        out_specs.append(pl.BlockSpec((rows, width), lambda j: (0, 0)))
    else:
        in_specs.append(pl.BlockSpec(memory_space=pl.ANY))
        operands.append(window)
        aliases = {len(operands) - 1: 0}
    return pl.pallas_call(
        body,
        grid=(steps,),
        in_specs=in_specs,
        out_specs=out_specs,
        out_shape=shapes,
        scratch_shapes=[pltpu.VMEM((count * rows, width), jnp.bfloat16)],
        input_output_aliases=aliases,
        compiler_params=pltpu.CompilerParams(vmem_limit_bytes=LIMIT),
        cost_estimate=pl.CostEstimate(
            flops=2 * count * rows * width * wide,
            transcendentals=count * rows,
            bytes_accessed=2 * width * wide + 6 * count * rows * width,
        ),
        name="kv_tiles",
    )(*operands)


def attend(slots, normed, w_blocks, gains, window):
    rows, width = normed.shape
    inner = gains.shape[1]
    cols = HEAD_GROUP * HEAD_DIM
    groups = inner // cols
    part = width // Y
    factor = math.log2(math.e) / math.sqrt(HEAD_DIM)

    def body(slot_ref, normed_ref, *refs):
        w_refs = refs[: len(w_blocks)]
        gain_ref, k_ref, v_ref, out_ref, w_all = refs[len(w_blocks) :]
        own_y = slot_ref[0]
        for w_ref, (shift, low) in zip(w_refs, [b[1:] for b in w_blocks], strict=True):
            at = pl.multiple_of(((own_y + shift) % Y) * part + low, 64)
            w_all[pl.ds(at, w_ref.shape[0]), :] = w_ref[...]
        raw = jnp.dot(normed_ref[...], w_all[...], preferred_element_type=jnp.float32)
        query = head_norm(raw, gain_ref[...])

        def heads(live):
            for h in range(HEAD_GROUP):
                span = slice(h * HEAD_DIM, (h + 1) * HEAD_DIM)
                q = query[:, span]
                scores = []
                for j in range(live):
                    k = k_ref[slot_ref[2 + j], :, span]
                    scores.append(
                        lax.dot_general(
                            q, k, (((1,), (1,)), ((), ())), preferred_element_type=jnp.float32
                        )
                    )
                highest = jnp.max(scores[0], axis=-1, keepdims=True)
                for s in scores[1:]:
                    highest = jnp.maximum(highest, jnp.max(s, axis=-1, keepdims=True))
                total = None
                mixed = None
                for j in range(live):
                    p = jnp.exp2((scores[j] - highest) * factor)
                    line = jnp.sum(p, axis=-1, keepdims=True)
                    v = v_ref[slot_ref[2 + j], :, span]
                    term = jnp.dot(p.astype(jnp.bfloat16), v, preferred_element_type=jnp.float32)
                    total = line if total is None else total + line
                    mixed = term if mixed is None else mixed + term
                out_ref[:, span] = (mixed * (1.0 / total)).astype(jnp.bfloat16)

        for live in range(2, NB + 1):

            @pl.when(slot_ref[1] == live)
            def _(live=live):
                heads(live)

    tiles = window.shape[0]
    in_specs = [pl.BlockSpec((rows, width), lambda g, s: (0, 0))]
    in_specs += [pl.BlockSpec((b[0].shape[0], cols), lambda g, s: (0, g)) for b in w_blocks]
    in_specs += [
        pl.BlockSpec((1, cols), lambda g, s: (0, g)),
        pl.BlockSpec((tiles, rows, cols), lambda g, s: (0, 0, g)),
        pl.BlockSpec((tiles, rows, cols), lambda g, s: (0, 0, groups + g)),
    ]
    return pl.pallas_call(
        body,
        grid_spec=pltpu.PrefetchScalarGridSpec(
            num_scalar_prefetch=1,
            grid=(groups,),
            in_specs=in_specs,
            out_specs=pl.BlockSpec((rows, cols), lambda g, s: (0, g)),
            scratch_shapes=[pltpu.VMEM((width, cols), jnp.bfloat16)],
        ),
        out_shape=jax.ShapeDtypeStruct((rows, inner), jnp.bfloat16),
        compiler_params=pltpu.CompilerParams(vmem_limit_bytes=LIMIT),
        cost_estimate=pl.CostEstimate(
            flops=2 * rows * width * inner + 4 * NB * rows * rows * inner,
            transcendentals=NB * rows * rows * HEADS,
            bytes_accessed=2 * width * inner + 4 * tiles * rows * inner,
        ),
        name="attend",
    )(slots, normed, *[b[0] for b in w_blocks], gains, window, window)


def project(attended, w_out, gate, residual, at, count):
    inner = attended.shape[1]
    width = w_out.shape[1]
    cols = 512

    def body(a_ref, w_ref, gate_ref, x_ref, out_ref):
        branch = jnp.dot(a_ref[...], w_ref[...], preferred_element_type=jnp.float32)
        out_ref[...] = (x_ref[...].astype(jnp.float32) + gate_ref[...] * branch).astype(
            jnp.bfloat16
        )

    block = at // count
    return pl.pallas_call(
        body,
        grid=(width // cols,),
        in_specs=[
            pl.BlockSpec((count, inner), lambda j: (block, 0)),
            pl.BlockSpec((inner, cols), lambda j: (0, j)),
            pl.BlockSpec((1, cols), lambda j: (0, j)),
            pl.BlockSpec((count, cols), lambda j: (block, j)),
        ],
        out_specs=pl.BlockSpec((count, cols), lambda j: (0, j)),
        out_shape=jax.ShapeDtypeStruct((count, width), jnp.bfloat16),
        compiler_params=pltpu.CompilerParams(vmem_limit_bytes=LIMIT),
        cost_estimate=pl.CostEstimate(
            flops=2 * count * inner * width,
            transcendentals=0,
            bytes_accessed=2 * inner * width + 6 * count * width,
        ),
        name="project",
    )(attended, w_out, gate, residual)


def gather_z(shard, z):
    rows, width = shard.shape
    block = jnp.zeros((Z, rows, width), shard.dtype)

    def put(block, piece, k):
        return lax.dynamic_update_slice(block, piece[None], ((z + k) % Z, 0, 0))

    block = put(block, shard, 0)
    up = down = shard
    for k in range(1, Z // 2 + 1):
        up = along_z(up, 1)
        block = put(block, up, Z - k)
        if k < Z - Z // 2:
            down = along_z(down, -1)
            block = put(block, down, k)
    return block.reshape(Z * rows, width)


def on_device(arriving, modulation, gate, w_query, w_kv, w_out, qk_gain, neighbors, live):
    x = arriving[0, 0]
    rows = x.shape[0]
    position = lax.axis_index("patch")
    y, z = position // Z, position % Z

    out_full = lax.all_gather(w_out[0], "patch", axis=0, tiled=True)
    up1, down1 = shifted(x, 1), shifted(x, -1)
    query_block = gather_z(w_query[0], z)
    half = query_block.shape[0] // 2
    w_blocks = [
        (query_block, 0, 0),
        (along_y(query_block, 1), Y - 1, 0),
        (along_y(query_block, -1), 1, 0),
        (along_y(query_block[:half], 2), Y - 2, 0),
        (along_y(query_block[half:], -2), 2, half),
    ]
    up2, down2 = shifted(up1, 1), shifted(down1, -1)

    window, normed = kv_tiles([x], modulation[0], w_kv[0], qk_gain[0, 1:2], 2 * SPAN, None)
    (window,) = kv_tiles([up1, down1], modulation[0], w_kv[0], qk_gain[0, 1:2], 0, window)
    (window,) = kv_tiles([up2, down2], modulation[0], w_kv[0], qk_gain[0, 1:2], 2, window)

    away = neighbors[0] - position
    place = jnp.where(away < 0, -2 * away - 2, 2 * away - 1)
    place = jnp.where(away == 0, 2 * SPAN, jnp.clip(place, 0, 2 * SPAN))
    slots = jnp.concatenate([y[None], live, place]).astype(jnp.int32)
    attended = attend(slots, normed, w_blocks, qk_gain[0, 0:1], window)
    count = rows // 2
    parts = [
        to_next_section(project(attended, out_full, gate, x, at, count)) for at in (0, count)
    ]
    return jnp.concatenate(parts, axis=0)[None, None]


def solution(mesh):
    placed = (
        P("section", "patch", None, None),
        P("section", None, None),
        P("section", None),
        P("section", "patch", None),
        P("section", None, None),
        P("section", "patch", None),
        P("section", None, None),
        P("patch", None),
        P("patch"),
    )
    return jax.shard_map(
        on_device,
        mesh=mesh,
        in_specs=placed,
        out_specs=P("section", "patch", None, None),
        check_vma=False,
    )
```

```python
import math

import jax
import jax.numpy as jnp
from jax import lax
from jax.experimental import pallas as pl
from jax.experimental.pallas import tpu as pltpu
from jax.sharding import PartitionSpec as P

HEADS = 12
HEAD_DIM = 128
SPAN = 2
NB = 4
Y, Z = 4, 8
COLS = 512
SMALL = 12 * 1024 * 1024
LARGE = 20 * 1024 * 1024
VMEM = pl.BlockSpec(memory_space=pltpu.VMEM)
SMEM = pl.BlockSpec(memory_space=pltpu.SMEM)
AT_Y, AT_Z, AT_LIVE, AT_SLOT, AT_NEED = 0, 1, 2, 3, 7


def shifted(value, steps):
    count = Y * Z
    return lax.ppermute(
        value, "patch", [(i, i + steps) for i in range(count) if 0 <= i + steps < count]
    )


def along_z(value, steps):
    return lax.ppermute(
        value, "patch", [(y * Z + z, y * Z + (z + steps) % Z) for y in range(Y) for z in range(Z)]
    )


def along_y(value, steps):
    return lax.ppermute(
        value, "patch", [(y * Z + z, ((y + steps) % Y) * Z + z) for y in range(Y) for z in range(Z)]
    )


def to_next_section(block):
    count = lax.axis_size("section")
    return lax.ppermute(block, "section", [(i, (i + 1) % count) for i in range(count)])


def norm_rows(x, modulation):
    values = x.astype(jnp.float32)
    width = values.shape[1]
    average = jnp.sum(values, axis=-1, keepdims=True) * (1.0 / width)
    centered = values - average
    variance = jnp.sum(centered * centered, axis=-1, keepdims=True) * (1.0 / width)
    scaled = centered * lax.rsqrt(variance + 1e-06)
    return (scaled * (1.0 + modulation[1:2]) + modulation[0:1]).astype(jnp.bfloat16)


def head_norm(raw, gains):
    parts = []
    for h in range(raw.shape[1] // HEAD_DIM):
        piece = raw[:, h * HEAD_DIM : (h + 1) * HEAD_DIM]
        square = jnp.sum(piece * piece, axis=-1, keepdims=True) * (1.0 / HEAD_DIM)
        gain = gains[:, h * HEAD_DIM : (h + 1) * HEAD_DIM]
        parts.append((piece * lax.rsqrt(square + 1e-06) * gain).astype(jnp.bfloat16))
    return jnp.concatenate(parts, axis=1) if len(parts) > 1 else parts[0]


def kernel(body, name, specs, shapes, scratch, aliases, flops, limit, operands):
    moved = sum(o.size * o.dtype.itemsize for o in operands)
    return pl.pallas_call(
        body,
        in_specs=specs,
        out_specs=[VMEM for _ in shapes],
        out_shape=shapes,
        scratch_shapes=scratch,
        input_output_aliases=aliases,
        compiler_params=pltpu.CompilerParams(vmem_limit_bytes=limit),
        cost_estimate=pl.CostEstimate(flops=flops, transcendentals=0, bytes_accessed=moved),
        name=name,
    )(*operands)


def project_kv(normed, w_ref, gain_ref, window_ref, tile):
    half = w_ref.shape[1] // 2

    @pl.loop(0, half // COLS)
    def _(j):
        cols = pl.ds(pl.multiple_of(j * COLS, COLS), COLS)
        raw = jnp.dot(normed[...], w_ref[:, cols], preferred_element_type=jnp.float32)
        window_ref[tile, :, cols] = head_norm(raw, gain_ref[:, cols])
        cols = pl.ds(pl.multiple_of(half + j * COLS, COLS), COLS)
        raw = jnp.dot(normed[...], w_ref[:, cols], preferred_element_type=jnp.float32)
        window_ref[tile, :, cols] = raw.astype(jnp.bfloat16)


def own_tile(x, modulation, w_kv, gains):
    rows, width = x.shape
    wide = w_kv.shape[1]

    def body(x_ref, modulation_ref, w_ref, gain_ref, window_ref, normed_ref):
        normed_ref[...] = norm_rows(x_ref[...], modulation_ref)
        project_kv(normed_ref, w_ref, gain_ref, window_ref, 2 * SPAN)

    shapes = [
        jax.ShapeDtypeStruct((2 * SPAN + 1, rows, wide), jnp.bfloat16),
        jax.ShapeDtypeStruct((rows, width), jnp.bfloat16),
    ]
    flops = 2 * rows * width * wide
    operands = [x, modulation, w_kv, gains]
    return kernel(body, "own_tile", [VMEM] * 4, shapes, [], {}, flops, SMALL, operands)


def near_tiles(scalars, tiles, modulation, w_kv, gains, window, start):
    count = len(tiles)
    rows, width = tiles[0].shape
    wide = w_kv.shape[1]

    def body(*refs):
        scalar_ref, x_refs = refs[0], refs[1 : 1 + count]
        modulation_ref, w_ref, gain_ref, _, window_ref, normed = refs[1 + count :]
        for i in range(count):

            @pl.when(scalar_ref[AT_NEED + start + i] > 0)
            def _(i=i):
                normed[i] = norm_rows(x_refs[i][...], modulation_ref)

        @pl.loop(0, count)
        def _(i):
            @pl.when(scalar_ref[AT_NEED + start + i] > 0)
            def _():
                project_kv(normed.at[i], w_ref, gain_ref, window_ref, start + i)

    shapes = [jax.ShapeDtypeStruct(window.shape, window.dtype)]
    specs = [SMEM] + [VMEM] * (count + 4)
    scratch = [pltpu.VMEM((count, rows, width), jnp.bfloat16)]
    operands = [scalars, *tiles, modulation, w_kv, gains, window]
    flops = 2 * count * rows * width * wide
    return kernel(
        body, "near_tiles", specs, shapes, scratch, {len(operands) - 1: 0}, flops, SMALL, operands
    )[0]


def place_rows(scalar_ref, sources, plan, low, size, target):
    for ref, (dy, zs, at) in zip(sources, plan, strict=True):
        at_y = (scalar_ref[AT_Y] + dy) % Y
        for k, dz in enumerate(zs):
            shard = at_y * Z + (scalar_ref[AT_Z] + dz) % Z
            row = pl.multiple_of(shard * size, 16)
            begin = at + k * 2 * size + low
            target[pl.ds(row, size), :] = ref[begin : begin + size, :]


def join(parts):
    count = parts[0].shape[0]

    def body(*refs):
        for k, ref in enumerate(refs[:-1]):
            refs[-1][k * count : (k + 1) * count, :] = ref[...]

    shape = (len(parts) * count, parts[0].shape[1])
    shapes = [jax.ShapeDtypeStruct(shape, parts[0].dtype)]
    return kernel(body, "join", [VMEM] * len(parts), shapes, [], {}, 1, SMALL, parts)[0]


def project_query(scalars, normed, gains, pieces, plan, size):
    rows, width = normed.shape
    inner = gains.shape[1]

    def body(scalar_ref, normed_ref, gain_ref, *refs):
        sources, (out_ref, whole) = refs[: len(pieces)], refs[len(pieces) :]
        place_rows(scalar_ref, sources, plan, 0, size, whole)
        for j in range(inner // COLS):
            cols = slice(j * COLS, (j + 1) * COLS)
            raw = jnp.dot(normed_ref[...], whole[:, cols], preferred_element_type=jnp.float32)
            out_ref[:, cols] = head_norm(raw, gain_ref[:, cols])

    shapes = [jax.ShapeDtypeStruct((rows, inner), jnp.bfloat16)]
    scratch = [pltpu.VMEM((width, inner), jnp.bfloat16)]
    specs = [SMEM] + [VMEM] * (2 + len(pieces))
    operands = [scalars, normed, gains, *pieces]
    flops = 2 * rows * width * inner
    return kernel(body, "project_query", specs, shapes, scratch, {}, flops, SMALL, operands)[0]


def whole_out(scalars, pieces, plan, size):
    width = pieces[0].shape[1]

    def body(scalar_ref, *refs):
        place_rows(scalar_ref, refs[: len(pieces)], plan, size, size, refs[-1])

    shapes = [jax.ShapeDtypeStruct((Y * Z * size, width), jnp.bfloat16)]
    specs = [SMEM] + [VMEM] * len(pieces)
    return kernel(body, "whole_out", specs, shapes, [], {}, 1, SMALL, [scalars, *pieces])[0]


def attend(scalars, query, window):
    rows, inner = query.shape
    factor = math.log2(math.e) / math.sqrt(HEAD_DIM)

    def body(scalar_ref, q_ref, window_ref, out_ref):
        def head(h, live):
            begin = pl.multiple_of(h * HEAD_DIM, HEAD_DIM)
            cols = pl.ds(begin, HEAD_DIM)
            value_cols = pl.ds(begin + inner, HEAD_DIM)
            q = q_ref[:, cols]
            scores = []
            for j in range(live):
                keys = window_ref[scalar_ref[AT_SLOT + j], :, cols]
                scores.append(
                    lax.dot_general(
                        q, keys, (((1,), (1,)), ((), ())), preferred_element_type=jnp.float32
                    )
                )
            highest = jnp.max(scores[0], axis=-1, keepdims=True)
            for s in scores[1:]:
                highest = jnp.maximum(highest, jnp.max(s, axis=-1, keepdims=True))
            total = mixed = None
            for j in range(live):
                p = jnp.exp2((scores[j] - highest) * factor)
                line = jnp.sum(p, axis=-1, keepdims=True)
                values = window_ref[scalar_ref[AT_SLOT + j], :, value_cols]
                term = jnp.dot(p.astype(jnp.bfloat16), values, preferred_element_type=jnp.float32)
                total = line if total is None else total + line
                mixed = term if mixed is None else mixed + term
            out_ref[:, cols] = (mixed * (1.0 / total)).astype(jnp.bfloat16)

        for live in range(2, NB + 1):

            @pl.when(scalar_ref[AT_LIVE] == live)
            def _(live=live):
                @pl.loop(0, HEADS // 2)
                def _(pair):
                    head(2 * pair, live)
                    head(2 * pair + 1, live)

    shapes = [jax.ShapeDtypeStruct((rows, inner), jnp.bfloat16)]
    flops = 4 * NB * rows * rows * inner
    operands = [scalars, query, window]
    specs = [SMEM, VMEM, VMEM]
    return kernel(body, "attend", specs, shapes, [], {}, flops, LARGE, operands)[0]


def project_out(attended, w_out, gate, x, at, count):
    width = w_out.shape[1]

    def body(a_ref, w_ref, gate_ref, x_ref, out_ref):
        for j in range(width // COLS):
            cols = slice(j * COLS, (j + 1) * COLS)
            branch = jnp.dot(
                a_ref[at : at + count, :], w_ref[:, cols], preferred_element_type=jnp.float32
            )
            residual = x_ref[at : at + count, cols].astype(jnp.float32)
            out_ref[:, cols] = (residual + gate_ref[:, cols] * branch).astype(jnp.bfloat16)

    shapes = [jax.ShapeDtypeStruct((count, width), jnp.bfloat16)]
    flops = 2 * count * width * w_out.shape[0]
    operands = [attended, w_out, gate, x]
    return kernel(body, "project_out", [VMEM] * 4, shapes, [], {}, flops, SMALL, operands)[0]


def on_device(arriving, modulation, gate, w_query, w_kv, w_out, qk_gain, neighbors, live):
    x = arriving[0, 0]
    rows = x.shape[0]
    size = w_query.shape[1]
    position = lax.axis_index("patch")
    away = neighbors[0] - position
    place = jnp.where(away < 0, -2 * away - 2, 2 * away - 1)
    place = jnp.where(away == 0, 2 * SPAN, jnp.clip(place, 0, 2 * SPAN))
    used = jnp.arange(NB, dtype=jnp.int32) < live[0]
    spots = jnp.arange(2 * SPAN, dtype=jnp.int32)
    need = jnp.any((place[:, None] == spots[None, :]) & used[:, None], axis=0)
    scalars = jnp.concatenate(
        [jnp.stack([position // Z, position % Z]), live, place, need.astype(jnp.int32)]
    ).astype(jnp.int32)

    shard = jnp.concatenate([w_query[0], w_out[0]], axis=0)
    up, down = [shard], [shard]
    for k in range(1, Z // 2 + 1):
        up.append(along_z(up[-1], 1))
        if k < Z // 2:
            down.append(along_z(down[-1], -1))
    low1, high1 = shifted(x, 1), shifted(x, -1)
    low2, high2 = shifted(low1, 1), shifted(high1, -1)
    groups = [
        ([-2, -1, 0, 1], [up[2], up[1], shard, down[1]], 1),
        ([-4, -3, 3, 2], [up[4], up[3], down[3], down[2]], -1),
    ]
    pieces, plan = [], []
    for zs, parts, onward in groups:
        block = join(parts)
        beside = {step: along_y(block, step) for step in (onward, -onward)}
        pieces += [block, beside[1], beside[-1], along_y(beside[onward], onward)]
        plan += [(0, zs, 0), (Y - 1, zs, 0), (1, zs, 0), (2, zs, 0)]

    gains = qk_gain[0]
    window, normed = own_tile(x, modulation[0], w_kv[0], gains[1:2])
    window = near_tiles(scalars, [low1, high1], modulation[0], w_kv[0], gains[1:2], window, 0)
    window = near_tiles(scalars, [low2, high2], modulation[0], w_kv[0], gains[1:2], window, 2)
    query = project_query(scalars, normed, gains[0:1], pieces, plan, size)
    out_whole = whole_out(scalars, pieces, plan, size)
    attended = attend(scalars, query, window)
    count = rows // 2
    parts = [
        to_next_section(project_out(attended, out_whole, gate, x, at, count)) for at in (0, count)
    ]
    return jnp.concatenate(parts, axis=0)[None, None]


def solution(mesh):
    placed = (
        P("section", "patch", None, None),
        P("section", None, None),
        P("section", None),
        P("section", "patch", None),
        P("section", None, None),
        P("section", "patch", None),
        P("section", None, None),
        P("patch", None),
        P("patch"),
    )
    return jax.shard_map(
        on_device,
        mesh=mesh,
        in_specs=placed,
        out_specs=P("section", "patch", None, None),
        check_vma=False,
    )
```

```python
import math

import jax
import jax.numpy as jnp
from jax import lax
from jax.experimental import pallas as pl
from jax.experimental.pallas import tpu as pltpu
from jax.sharding import PartitionSpec as P

HEADS = 12
HEAD_DIM = 128
SPAN = 2
NB = 4
Y, Z = 4, 8
COLS = 512
SMALL = 12 * 1024 * 1024
LARGE = 20 * 1024 * 1024
VMEM = pl.BlockSpec(memory_space=pltpu.VMEM)
SMEM = pl.BlockSpec(memory_space=pltpu.SMEM)
HBM = pl.BlockSpec(memory_space=pltpu.HBM)
OFFSETS = [-1, 1, -2, 2]


def along_z(value, steps, wrap=True):
    pairs = [
        (y * Z + z, y * Z + (z + steps) % Z)
        for y in range(Y)
        for z in range(Z)
        if wrap or 0 <= z + steps < Z
    ]
    return lax.ppermute(value, "patch", pairs)


def around_rows(value):
    ends = [(y * Z + Z - 1, (y + 1) * Z) for y in range(Y - 1)]
    return lax.ppermute(value, "patch", ends + [(b, a) for a, b in ends])


def along_y(value, steps):
    return lax.ppermute(
        value, "patch", [(y * Z + z, ((y + steps) % Y) * Z + z) for y in range(Y) for z in range(Z)]
    )


def along_y_by_half(value, steps):
    pairs = [
        (y * Z + z, ((y + (steps if z < Z // 2 else -steps)) % Y) * Z + z)
        for y in range(Y)
        for z in range(Z)
    ]
    return lax.ppermute(value, "patch", pairs)


def across_rows(value):
    pairs = [(y * Z + Z - 1, (y + 1) * Z + Z - 1) for y in range(Y - 1)]
    pairs += [((y + 1) * Z, y * Z) for y in range(Y - 1)]
    return lax.ppermute(value, "patch", pairs)


def to_next_section(block):
    count = lax.axis_size("section")
    return lax.ppermute(block, "section", [(i, (i + 1) % count) for i in range(count)])


def norm_rows(x, modulation):
    values = x.astype(jnp.float32)
    width = values.shape[1]
    average = jnp.sum(values, axis=-1, keepdims=True) * (1.0 / width)
    centered = values - average
    variance = jnp.sum(centered * centered, axis=-1, keepdims=True) * (1.0 / width)
    scaled = centered * lax.rsqrt(variance + 1e-06)
    return (scaled * (1.0 + modulation[1:2]) + modulation[0:1]).astype(jnp.bfloat16)


def head_norm(raw, gains):
    parts = []
    for h in range(raw.shape[1] // HEAD_DIM):
        piece = raw[:, h * HEAD_DIM : (h + 1) * HEAD_DIM]
        square = jnp.sum(piece * piece, axis=-1, keepdims=True) * (1.0 / HEAD_DIM)
        gain = gains[:, h * HEAD_DIM : (h + 1) * HEAD_DIM]
        parts.append((piece * lax.rsqrt(square + 1e-06) * gain).astype(jnp.bfloat16))
    return jnp.concatenate(parts, axis=1) if len(parts) > 1 else parts[0]


def kernel(body, name, specs, shapes, scratch, aliases, flops, limit, operands):
    moved = sum(o.size * o.dtype.itemsize for o in operands)
    return pl.pallas_call(
        body,
        in_specs=specs,
        out_specs=[VMEM for _ in shapes],
        out_shape=shapes,
        scratch_shapes=scratch,
        input_output_aliases=aliases,
        compiler_params=pltpu.CompilerParams(vmem_limit_bytes=limit),
        cost_estimate=pl.CostEstimate(flops=flops, transcendentals=0, bytes_accessed=moved),
        name=name,
    )(*operands)


def after(value, *others):
    return lax.optimization_barrier((value, *others))[0]


def own_tile(x, modulation, w_kv, gains):
    rows, width = x.shape
    wide = w_kv.shape[1]
    steps = wide // COLS

    def body(x_hbm, modulation_ref, w_hbm, gain_ref, window_ref, normed_ref, w_ref, x_ref, sems):
        def fetch(j):
            cols = pl.ds(pl.multiple_of(j * COLS, COLS), COLS)
            return pltpu.make_async_copy(w_hbm.at[:, cols], w_ref.at[:, cols], sems.at[j])

        rows_in = pltpu.make_async_copy(x_hbm, x_ref, sems.at[steps])
        rows_in.start()
        for j in range(steps):
            fetch(j).start()
        rows_in.wait()
        normed_ref[...] = norm_rows(x_ref[...], modulation_ref)

        @pl.loop(0, steps // 2)
        def _(j):
            fetch(j).wait()
            cols = pl.ds(pl.multiple_of(j * COLS, COLS), COLS)
            raw = jnp.dot(normed_ref[...], w_ref[:, cols], preferred_element_type=jnp.float32)
            window_ref[2 * SPAN, :, cols] = head_norm(raw, gain_ref[:, cols])

        @pl.loop(steps // 2, steps)
        def _(j):
            fetch(j).wait()
            cols = pl.ds(pl.multiple_of(j * COLS, COLS), COLS)
            raw = jnp.dot(normed_ref[...], w_ref[:, cols], preferred_element_type=jnp.float32)
            window_ref[2 * SPAN, :, cols] = raw.astype(jnp.bfloat16)

    shapes = [
        jax.ShapeDtypeStruct((2 * SPAN + 1, rows, wide), jnp.bfloat16),
        jax.ShapeDtypeStruct((rows, width), jnp.bfloat16),
        jax.ShapeDtypeStruct(w_kv.shape, w_kv.dtype),
    ]
    scratch = [pltpu.VMEM((rows, width), x.dtype), pltpu.SemaphoreType.DMA((steps + 1,))]
    flops = 2 * rows * width * wide
    x, w_kv = (pltpu.with_memory_space_constraint(o, pltpu.HBM) for o in (x, w_kv))
    operands = [x, modulation, w_kv, gains]
    specs = [HBM, VMEM, HBM, VMEM]
    return kernel(body, "own_tile", specs, shapes, scratch, {}, flops, SMALL, operands)


def near_tile(place, scalars, tile, modulation, w_kv, gains, window):
    rows, width = tile.shape
    wide = w_kv.shape[1]

    def body(
        at_ref, list_ref, live_ref, x_ref, modulation_ref, w_ref, gain_ref, _, window_ref, normed
    ):
        named = False
        for j in range(1, NB):
            hit = (list_ref[j] - at_ref[0] == OFFSETS[place]) & (live_ref[0] > j)
            named = named | hit

        @pl.when(named)
        def _():
            normed[...] = norm_rows(x_ref[...], modulation_ref)

            @pl.loop(0, wide // (2 * COLS))
            def _(j):
                cols = pl.ds(pl.multiple_of(j * COLS, COLS), COLS)
                raw = jnp.dot(normed[...], w_ref[:, cols], preferred_element_type=jnp.float32)
                window_ref[place, :, cols] = head_norm(raw, gain_ref[:, cols])
                cols = pl.ds(pl.multiple_of(wide // 2 + j * COLS, COLS), COLS)
                raw = jnp.dot(normed[...], w_ref[:, cols], preferred_element_type=jnp.float32)
                window_ref[place, :, cols] = raw.astype(jnp.bfloat16)

    shapes = [jax.ShapeDtypeStruct(window.shape, window.dtype)]
    specs = [SMEM] * 3 + [VMEM] * 5
    scratch = [pltpu.VMEM((rows, width), jnp.bfloat16)]
    operands = [*scalars, tile, modulation, w_kv, gains, window]
    flops = 2 * rows * width * wide
    aliases = {len(operands) - 1: 0}
    return kernel(body, "near_tile", specs, shapes, scratch, aliases, flops, SMALL, operands)[0]


def join(parts):
    rows, width = parts[0].shape
    count = rows // 2

    def body(*refs):
        whole = refs[-1]
        second = count * len(parts)
        for k, ref in enumerate(refs[:-1]):
            whole[k * count : (k + 1) * count, :] = ref[:count, :]
            whole[second + k * count : second + (k + 1) * count, :] = ref[count:, :]

    shapes = [jax.ShapeDtypeStruct((len(parts) * rows, width), parts[0].dtype)]
    return kernel(body, "join", [VMEM] * len(parts), shapes, [], {}, 1, SMALL, parts)[0]


def onward(at, lows, highs):
    rows, width = lows[0].shape
    half = rows // 2
    count = len(lows)

    def body(at_ref, *refs):
        low_refs, high_refs, (query_ref, out_ref) = (
            refs[:count],
            refs[count : 2 * count],
            refs[2 * count :],
        )
        for left, query_from, out_from in (
            (True, high_refs, low_refs),
            (False, low_refs, high_refs),
        ):

            @pl.when((at_ref[0] % Z < Z // 2) == left)
            def _(query_from=query_from, out_from=out_from):
                for k in range(count):
                    query_ref[k * half : (k + 1) * half, :] = query_from[k][:half, :]
                    out_ref[k * half : (k + 1) * half, :] = out_from[k][half:, :]

    shapes = [jax.ShapeDtypeStruct((count * half, width), lows[0].dtype)] * 2
    specs = [SMEM] + [VMEM] * (2 * count)
    return kernel(body, "onward", specs, shapes, [], {}, 1, SMALL, [at, *lows, *highs])


def place_rows(at_ref, sources, plan, size, target):
    own_y, own_z = at_ref[0] // Z, at_ref[0] % Z
    for ref, (dy, zs, begin) in zip(sources, plan, strict=True):
        at_y = (own_y + dy) % Y
        for k, dz in enumerate(zs):
            shard = at_y * Z + (own_z + dz) % Z
            row = pl.multiple_of(shard * size, 16)
            target[pl.ds(row, size), :] = ref[begin + k * size : begin + (k + 1) * size, :]


def project_query(at, normed, gains, pieces, plan):
    rows, width = normed.shape
    inner = gains.shape[1]
    size = width // (Y * Z)

    def body(at_ref, normed_ref, gain_ref, *refs):
        sources, (out_ref, whole) = refs[: len(pieces)], refs[len(pieces) :]
        place_rows(at_ref, sources, plan, size, whole)
        for j in range(inner // COLS):
            cols = slice(j * COLS, (j + 1) * COLS)
            raw = jnp.dot(normed_ref[...], whole[:, cols], preferred_element_type=jnp.float32)
            out_ref[:, cols] = head_norm(raw, gain_ref[:, cols])

    shapes = [jax.ShapeDtypeStruct((rows, inner), jnp.bfloat16)]
    scratch = [pltpu.VMEM((width, inner), jnp.bfloat16)]
    specs = [SMEM] + [VMEM] * (2 + len(pieces))
    operands = [at, normed, gains, *pieces]
    flops = 2 * rows * width * inner
    return kernel(body, "project_query", specs, shapes, scratch, {}, flops, SMALL, operands)[0]


def whole_out(at, pieces, plan, inner):
    width = pieces[0].shape[1]
    size = inner // (Y * Z)

    def body(at_ref, *refs):
        place_rows(at_ref, refs[: len(pieces)], plan, size, refs[-1])

    shapes = [jax.ShapeDtypeStruct((inner, width), jnp.bfloat16)]
    specs = [SMEM] + [VMEM] * len(pieces)
    return kernel(body, "whole_out", specs, shapes, [], {}, 1, SMALL, [at, *pieces])[0]


def attend(scalars, query, window):
    rows, inner = query.shape
    factor = math.log2(math.e) / math.sqrt(HEAD_DIM)

    def body(at_ref, list_ref, live_ref, q_ref, window_ref, out_ref):
        def place(j):
            away = list_ref[j] - at_ref[0]
            found = jnp.where(away < 0, -2 * away - 2, 2 * away - 1)
            return jnp.where(away == 0, 2 * SPAN, jnp.clip(found, 0, 2 * SPAN - 1))

        def head(h, places):
            begin = pl.multiple_of(h * HEAD_DIM, HEAD_DIM)
            cols = pl.ds(begin, HEAD_DIM)
            value_cols = pl.ds(begin + inner, HEAD_DIM)
            q = q_ref[:, cols]
            scores = []
            for p in places:
                keys = window_ref[p, :, cols]
                scores.append(
                    lax.dot_general(
                        q, keys, (((1,), (1,)), ((), ())), preferred_element_type=jnp.float32
                    )
                )
            highest = jnp.max(scores[0], axis=-1, keepdims=True)
            for s in scores[1:]:
                highest = jnp.maximum(highest, jnp.max(s, axis=-1, keepdims=True))
            total = mixed = None
            for s, p in zip(scores, places, strict=True):
                weight = jnp.exp2((s - highest) * factor)
                line = jnp.sum(weight, axis=-1, keepdims=True)
                term = jnp.dot(
                    weight.astype(jnp.bfloat16),
                    window_ref[p, :, value_cols],
                    preferred_element_type=jnp.float32,
                )
                total = line if total is None else total + line
                mixed = term if mixed is None else mixed + term
            out_ref[:, cols] = (mixed * (1.0 / total)).astype(jnp.bfloat16)

        for live in range(2, NB + 1):

            @pl.when(live_ref[0] == live)
            def _(live=live):
                places = [2 * SPAN] + [place(j) for j in range(1, live)]

                @pl.loop(0, HEADS // 2)
                def _(pair):
                    head(2 * pair, places)
                    head(2 * pair + 1, places)

    shapes = [jax.ShapeDtypeStruct((rows, inner), jnp.bfloat16)]
    flops = 4 * NB * rows * rows * inner
    operands = [*scalars, query, window]
    specs = [SMEM] * 3 + [VMEM] * 2
    return kernel(body, "attend", specs, shapes, [], {}, flops, LARGE, operands)[0]


def project_out(attended, w_out, gate, x, at, count):
    width = w_out.shape[1]

    def body(a_ref, w_ref, gate_ref, x_ref, out_ref):
        for j in range(width // COLS):
            cols = slice(j * COLS, (j + 1) * COLS)
            branch = jnp.dot(
                a_ref[at : at + count, :], w_ref[:, cols], preferred_element_type=jnp.float32
            )
            residual = x_ref[at : at + count, cols].astype(jnp.float32)
            out_ref[:, cols] = (residual + gate_ref[:, cols] * branch).astype(jnp.bfloat16)

    shapes = [jax.ShapeDtypeStruct((count, width), jnp.bfloat16)]
    flops = 2 * count * width * w_out.shape[0]
    operands = [attended, w_out, gate, x]
    return kernel(body, "project_out", [VMEM] * 4, shapes, [], {}, flops, SMALL, operands)[0]


def on_device(arriving, modulation, gate, w_query, w_kv, w_out, qk_gain, neighbors, live):
    x = arriving[0, 0]
    rows = x.shape[0]
    at = lax.axis_index("patch").astype(jnp.int32).reshape(1)
    size = w_query.shape[1]
    scalars = [at, neighbors[0], live]
    gains = qk_gain[0]

    shard = jnp.concatenate([w_query[0], w_out[0]], axis=0)
    zs_a, zs_b = [-2, -1, 0, 1], [-4, -3, 3, 2]
    up, down = [shard], [shard]
    for k in range(1, 3):
        up.append(along_z(up[-1], 1))
        down.append(along_z(down[-1], -1))
    crossed = across_rows(x)
    own_z = at[0] % Z
    block_a = join([up[2], up[1], shard, down[1]])
    low_a, high_a = along_y(block_a, 1), along_y(block_a, -1)
    up.append(along_z(up[2], 1))
    down.append(along_z(down[2], -1))
    up.append(along_z(after(up[3], block_a), 1))
    block_b = join([up[4], up[3], down[3], down[2]])
    x_up = after(jnp.where(own_z == Z - 1, crossed, x), up[4], down[3])
    x_down = after(jnp.where(own_z == 0, crossed, x), up[4], down[3])
    low1, high1 = along_z(x_up, 1), along_z(x_down, -1)
    low_b = along_y(block_b, 1)
    window, normed, w_kv_near = own_tile(after(x, block_b), modulation[0], w_kv[0], gains[1:2])
    high_b = along_y(after(block_b, normed, low_a, high_a), -1)
    low2, high2 = along_z(low1, 1, wrap=False), along_z(high1, -1, wrap=False)

    def add_tile(window, place, tile):
        return near_tile(place, scalars, tile, modulation[0], w_kv_near, gains[1:2], window)

    window = add_tile(add_tile(window, 0, low1), 1, high1)
    low_b, high_b, window = lax.optimization_barrier((low_b, high_b, window))
    edge = after(jnp.where(own_z == 0, high1, low1), low_b)
    edge_far = around_rows(edge)
    query_on, out_on = onward(at, [low_a, after(low_b, edge)], [high_a, high_b])
    query_far = along_y_by_half(query_on, -1)
    out_far = along_y_by_half(out_on, 1)
    near_blocks = [block_a, low_a, high_a, block_b, low_b, high_b]
    sides = [(dy, zs) for zs in (zs_a, zs_b) for dy in (0, Y - 1, 1)]
    half = len(zs_a) * size
    query_plan = [(dy, zs, 0) for dy, zs in sides] + [(2, zs_a + zs_b, 0)]
    out_plan = [(dy, zs, half) for dy, zs in sides] + [(2, zs_a + zs_b, 0)]
    query_pieces = near_blocks + [query_far]
    out_pieces = near_blocks + [out_far]

    window = add_tile(window, 2, jnp.where(own_z == 0, edge_far, low2))
    window = add_tile(window, 3, jnp.where(own_z == Z - 1, edge_far, high2))
    query = project_query(at, normed, gains[0:1], query_pieces, query_plan)
    out_whole = whole_out(at, out_pieces, out_plan, gains.shape[1])
    attended = attend(scalars, query, window)
    count = rows // 2
    parts = [
        to_next_section(project_out(attended, out_whole, gate, x, at_row, count))
        for at_row in (0, count)
    ]
    return jnp.concatenate(parts, axis=0)[None, None]


def solution(mesh):
    placed = (
        P("section", "patch", None, None),
        P("section", None, None),
        P("section", None),
        P("section", "patch", None),
        P("section", None, None),
        P("section", "patch", None),
        P("section", None, None),
        P("patch", None),
        P("patch"),
    )
    return jax.shard_map(
        on_device,
        mesh=mesh,
        in_specs=placed,
        out_specs=P("section", "patch", None, None),
        check_vma=False,
    )
```

```python
import math

import jax
import jax.numpy as jnp
from jax import lax
from jax.experimental import pallas as pl
from jax.experimental.pallas import tpu as pltpu
from jax.sharding import PartitionSpec as P

HEADS = 12
HEAD_DIM = 128
SPAN = 2
NB = 4
Y, Z = 4, 8
COLS = 512
SMALL = 12 * 1024 * 1024
LARGE = 20 * 1024 * 1024
VMEM = pl.BlockSpec(memory_space=pltpu.VMEM)
SMEM = pl.BlockSpec(memory_space=pltpu.SMEM)
HBM = pl.BlockSpec(memory_space=pltpu.HBM)
OFFSETS = [-1, 1, -2, 2]


def along_z(value, steps, wrap=True):
    pairs = [
        (y * Z + z, y * Z + (z + steps) % Z)
        for y in range(Y)
        for z in range(Z)
        if wrap or 0 <= z + steps < Z
    ]
    return lax.ppermute(value, "patch", pairs)


def around_rows(value):
    ends = [(y * Z + Z - 1, (y + 1) * Z) for y in range(Y - 1)]
    return lax.ppermute(value, "patch", ends + [(b, a) for a, b in ends])


def along_y(value, steps):
    return lax.ppermute(
        value, "patch", [(y * Z + z, ((y + steps) % Y) * Z + z) for y in range(Y) for z in range(Z)]
    )


def along_y_by_place(value, steps):
    pairs = [(y * Z + z, ((y + steps[z]) % Y) * Z + z) for y in range(Y) for z in range(Z)]
    return lax.ppermute(value, "patch", pairs)


def across_rows(value):
    pairs = [(y * Z + Z - 1, (y + 1) * Z + Z - 1) for y in range(Y - 1)]
    pairs += [((y + 1) * Z, y * Z) for y in range(Y - 1)]
    return lax.ppermute(value, "patch", pairs)


def to_next_section(block):
    count = lax.axis_size("section")
    return lax.ppermute(block, "section", [(i, (i + 1) % count) for i in range(count)])


def norm_rows(x, modulation):
    values = x.astype(jnp.float32)
    width = values.shape[1]
    average = jnp.sum(values, axis=-1, keepdims=True) * (1.0 / width)
    centered = values - average
    variance = jnp.sum(centered * centered, axis=-1, keepdims=True) * (1.0 / width)
    scaled = centered * lax.rsqrt(variance + 1e-06)
    return (scaled * (1.0 + modulation[1:2]) + modulation[0:1]).astype(jnp.bfloat16)


def head_norm(raw, gains):
    parts = []
    for h in range(raw.shape[1] // HEAD_DIM):
        piece = raw[:, h * HEAD_DIM : (h + 1) * HEAD_DIM]
        square = jnp.sum(piece * piece, axis=-1, keepdims=True) * (1.0 / HEAD_DIM)
        gain = gains[:, h * HEAD_DIM : (h + 1) * HEAD_DIM]
        parts.append((piece * lax.rsqrt(square + 1e-06) * gain).astype(jnp.bfloat16))
    return jnp.concatenate(parts, axis=1) if len(parts) > 1 else parts[0]


def kernel(body, name, specs, shapes, scratch, aliases, flops, limit, operands):
    moved = sum(o.size * o.dtype.itemsize for o in operands)
    return pl.pallas_call(
        body,
        in_specs=specs,
        out_specs=[VMEM for _ in shapes],
        out_shape=shapes,
        scratch_shapes=scratch,
        input_output_aliases=aliases,
        compiler_params=pltpu.CompilerParams(vmem_limit_bytes=limit),
        cost_estimate=pl.CostEstimate(flops=flops, transcendentals=0, bytes_accessed=moved),
        name=name,
    )(*operands)


def after(value, *others):
    return lax.optimization_barrier((value, *others))[0]


def own_tile(x, modulation, w_kv, gains):
    rows, width = x.shape
    wide = w_kv.shape[1]
    steps = wide // COLS

    def body(x_hbm, modulation_ref, w_hbm, gain_ref, window_ref, normed_ref, w_ref, x_ref, sems):
        def fetch(j):
            cols = pl.ds(pl.multiple_of(j * COLS, COLS), COLS)
            return pltpu.make_async_copy(w_hbm.at[:, cols], w_ref.at[:, cols], sems.at[j])

        rows_in = pltpu.make_async_copy(x_hbm, x_ref, sems.at[steps])
        rows_in.start()
        for j in range(steps):
            fetch(j).start()
        rows_in.wait()
        normed_ref[...] = norm_rows(x_ref[...], modulation_ref)

        @pl.loop(0, steps // 2)
        def _(j):
            fetch(j).wait()
            cols = pl.ds(pl.multiple_of(j * COLS, COLS), COLS)
            raw = jnp.dot(normed_ref[...], w_ref[:, cols], preferred_element_type=jnp.float32)
            window_ref[2 * SPAN, :, cols] = head_norm(raw, gain_ref[:, cols])

        @pl.loop(steps // 2, steps)
        def _(j):
            fetch(j).wait()
            cols = pl.ds(pl.multiple_of(j * COLS, COLS), COLS)
            raw = jnp.dot(normed_ref[...], w_ref[:, cols], preferred_element_type=jnp.float32)
            window_ref[2 * SPAN, :, cols] = raw.astype(jnp.bfloat16)

    shapes = [
        jax.ShapeDtypeStruct((2 * SPAN + 1, rows, wide), jnp.bfloat16),
        jax.ShapeDtypeStruct((rows, width), jnp.bfloat16),
        jax.ShapeDtypeStruct(w_kv.shape, w_kv.dtype),
    ]
    scratch = [pltpu.VMEM((rows, width), x.dtype), pltpu.SemaphoreType.DMA((steps + 1,))]
    flops = 2 * rows * width * wide
    x, w_kv = (pltpu.with_memory_space_constraint(o, pltpu.HBM) for o in (x, w_kv))
    operands = [x, modulation, w_kv, gains]
    specs = [HBM, VMEM, HBM, VMEM]
    return kernel(body, "own_tile", specs, shapes, scratch, {}, flops, SMALL, operands)


def near_tile(place, scalars, tile, modulation, w_kv, gains, window):
    rows, width = tile.shape
    wide = w_kv.shape[1]

    def body(
        at_ref, list_ref, live_ref, x_ref, modulation_ref, w_ref, gain_ref, _, window_ref, normed
    ):
        own_z = at_ref[0] % Z
        if place is None:
            spot = jnp.where(own_z == 0, 2, 3)
            offset = jnp.where(own_z == 0, OFFSETS[2], OFFSETS[3])
            here = (own_z == 0) | (own_z == Z - 1)
        else:
            spot, offset = place, OFFSETS[place]
            here = {0: True, 1: True, 2: own_z != 0, 3: own_z != Z - 1}[place]
        named = False
        for j in range(1, NB):
            named = named | ((list_ref[j] - at_ref[0] == offset) & (live_ref[0] > j))

        @pl.when(named & here)
        def _():
            normed[...] = norm_rows(x_ref[...], modulation_ref)

            @pl.loop(0, wide // (2 * COLS))
            def _(j):
                cols = pl.ds(pl.multiple_of(j * COLS, COLS), COLS)
                raw = jnp.dot(normed[...], w_ref[:, cols], preferred_element_type=jnp.float32)
                window_ref[spot, :, cols] = head_norm(raw, gain_ref[:, cols])
                cols = pl.ds(pl.multiple_of(wide // 2 + j * COLS, COLS), COLS)
                raw = jnp.dot(normed[...], w_ref[:, cols], preferred_element_type=jnp.float32)
                window_ref[spot, :, cols] = raw.astype(jnp.bfloat16)

    shapes = [jax.ShapeDtypeStruct(window.shape, window.dtype)]
    specs = [SMEM] * 3 + [VMEM] * 5
    scratch = [pltpu.VMEM((rows, width), jnp.bfloat16)]
    operands = [*scalars, tile, modulation, w_kv, gains, window]
    flops = 2 * rows * width * wide
    aliases = {len(operands) - 1: 0}
    return kernel(body, "near_tile", specs, shapes, scratch, aliases, flops, SMALL, operands)[0]


def join(parts):
    rows, width = parts[0].shape
    count = rows // 2

    def body(*refs):
        whole = refs[-1]
        second = count * len(parts)
        for k, ref in enumerate(refs[:-1]):
            whole[k * count : (k + 1) * count, :] = ref[:count, :]
            whole[second + k * count : second + (k + 1) * count, :] = ref[count:, :]

    shapes = [jax.ShapeDtypeStruct((len(parts) * rows, width), parts[0].dtype)]
    return kernel(body, "join", [VMEM] * len(parts), shapes, [], {}, 1, SMALL, parts)[0]


def onward(at, lows, highs):
    width = lows[0].shape[1]
    halves = [low.shape[0] // 2 for low in lows]
    begins = [sum(halves[:k]) for k in range(len(halves))]
    count = len(lows)

    def body(at_ref, *refs):
        low_refs, high_refs = refs[:count], refs[count : 2 * count]
        query_ref, out_refs = refs[2 * count], refs[2 * count + 1 :]
        own_z = at_ref[0] % Z
        left = own_z < Z // 2
        right = jnp.logical_not(left)
        end = (own_z == 0) | (own_z == Z - 1)
        for pick, source in ((left, high_refs), (right, low_refs)):

            @pl.when(pick)
            def _(source=source):
                for k, (begin, half) in enumerate(zip(begins, halves, strict=True)):
                    query_ref[begin : begin + half, :] = source[k][:half, :]

        for k, half in enumerate(halves):
            from_low = left if k < count - 1 else left != end
            for pick, source in ((from_low, low_refs), (jnp.logical_not(from_low), high_refs)):

                @pl.when(pick)
                def _(k=k, half=half, source=source):
                    out_refs[k][...] = source[k][half:, :]

    sizes = [sum(halves), *halves]
    shapes = [jax.ShapeDtypeStruct((n, width), lows[0].dtype) for n in sizes]
    specs = [SMEM] + [VMEM] * (2 * count)
    return kernel(body, "onward", specs, shapes, [], {}, 1, SMALL, [at, *lows, *highs])


def place_rows(at_ref, sources, plan, size, target):
    own_y, own_z = at_ref[0] // Z, at_ref[0] % Z
    for ref, (dy, zs, begin) in zip(sources, plan, strict=True):
        at_y = (own_y + dy) % Y
        for k, dz in enumerate(zs):
            shard = at_y * Z + (own_z + dz) % Z
            row = pl.multiple_of(shard * size, 16)
            target[pl.ds(row, size), :] = ref[begin + k * size : begin + (k + 1) * size, :]


def project_query(at, normed, gains, pieces, plan):
    rows, width = normed.shape
    inner = gains.shape[1]
    size = width // (Y * Z)

    def body(at_ref, normed_ref, gain_ref, *refs):
        sources, (out_ref, whole) = refs[: len(pieces)], refs[len(pieces) :]
        place_rows(at_ref, sources, plan, size, whole)
        for j in range(inner // COLS):
            cols = slice(j * COLS, (j + 1) * COLS)
            raw = jnp.dot(normed_ref[...], whole[:, cols], preferred_element_type=jnp.float32)
            out_ref[:, cols] = head_norm(raw, gain_ref[:, cols])

    shapes = [jax.ShapeDtypeStruct((rows, inner), jnp.bfloat16)]
    scratch = [pltpu.VMEM((width, inner), jnp.bfloat16)]
    specs = [SMEM] + [VMEM] * (2 + len(pieces))
    operands = [at, normed, gains, *pieces]
    flops = 2 * rows * width * inner
    return kernel(body, "project_query", specs, shapes, scratch, {}, flops, SMALL, operands)[0]


def whole_out(at, pieces, plan, inner):
    width = pieces[0].shape[1]
    size = inner // (Y * Z)

    def body(at_ref, *refs):
        place_rows(at_ref, refs[: len(pieces)], plan, size, refs[-1])

    shapes = [jax.ShapeDtypeStruct((inner, width), jnp.bfloat16)]
    specs = [SMEM] + [VMEM] * len(pieces)
    return kernel(body, "whole_out", specs, shapes, [], {}, 1, SMALL, [at, *pieces])[0]


def attend(scalars, query, window):
    rows, inner = query.shape
    factor = math.log2(math.e) / math.sqrt(HEAD_DIM)

    def body(at_ref, list_ref, live_ref, q_ref, window_ref, out_ref):
        def place(j):
            away = list_ref[j] - at_ref[0]
            found = jnp.where(away < 0, -2 * away - 2, 2 * away - 1)
            return jnp.where(away == 0, 2 * SPAN, jnp.clip(found, 0, 2 * SPAN - 1))

        def head(h, places):
            begin = pl.multiple_of(h * HEAD_DIM, HEAD_DIM)
            cols = pl.ds(begin, HEAD_DIM)
            value_cols = pl.ds(begin + inner, HEAD_DIM)
            q = q_ref[:, cols]
            scores = []
            for p in places:
                keys = window_ref[p, :, cols]
                scores.append(
                    lax.dot_general(
                        q, keys, (((1,), (1,)), ((), ())), preferred_element_type=jnp.float32
                    )
                )
            highest = jnp.max(scores[0], axis=-1, keepdims=True)
            for s in scores[1:]:
                highest = jnp.maximum(highest, jnp.max(s, axis=-1, keepdims=True))
            total = mixed = None
            for s, p in zip(scores, places, strict=True):
                weight = jnp.exp2((s - highest) * factor)
                line = jnp.sum(weight, axis=-1, keepdims=True)
                term = jnp.dot(
                    weight.astype(jnp.bfloat16),
                    window_ref[p, :, value_cols],
                    preferred_element_type=jnp.float32,
                )
                total = line if total is None else total + line
                mixed = term if mixed is None else mixed + term
            out_ref[:, cols] = (mixed * (1.0 / total)).astype(jnp.bfloat16)

        for live in range(2, NB + 1):

            @pl.when(live_ref[0] == live)
            def _(live=live):
                places = [2 * SPAN] + [place(j) for j in range(1, live)]

                @pl.loop(0, HEADS // 2)
                def _(pair):
                    head(2 * pair, places)
                    head(2 * pair + 1, places)

    shapes = [jax.ShapeDtypeStruct((rows, inner), jnp.bfloat16)]
    flops = 4 * rows * NB * window.shape[1] * inner
    operands = [*scalars, query, window]
    specs = [SMEM] * 3 + [VMEM] * 2
    return kernel(body, "attend", specs, shapes, [], {}, flops, LARGE, operands)[0]


def project_out(attended, w_out, gate, x, at, count):
    width = w_out.shape[1]

    def body(a_ref, w_ref, gate_ref, x_ref, out_ref):
        for j in range(width // COLS):
            cols = slice(j * COLS, (j + 1) * COLS)
            branch = jnp.dot(
                a_ref[at : at + count, :], w_ref[:, cols], preferred_element_type=jnp.float32
            )
            residual = x_ref[at : at + count, cols].astype(jnp.float32)
            out_ref[:, cols] = (residual + gate_ref[:, cols] * branch).astype(jnp.bfloat16)

    shapes = [jax.ShapeDtypeStruct((count, width), jnp.bfloat16)]
    flops = 2 * count * width * w_out.shape[0]
    operands = [attended, w_out, gate, x]
    return kernel(body, "project_out", [VMEM] * 4, shapes, [], {}, flops, SMALL, operands)[0]


def on_device(arriving, modulation, gate, w_query, w_kv, w_out, qk_gain, neighbors, live):
    x = arriving[0, 0]
    rows = x.shape[0]
    at = lax.axis_index("patch").astype(jnp.int32).reshape(1)
    size = w_query.shape[1]
    scalars = [at, neighbors[0], live]
    gains = qk_gain[0]

    shard = jnp.concatenate([w_query[0], w_out[0]], axis=0)
    zs_a, zs_b = [-2, -1, 0, 1, 2], [-4, -3, 3]
    up, down = [shard], [shard]
    for k in range(1, 3):
        up.append(along_z(up[-1], 1))
        down.append(along_z(down[-1], -1))
    crossed = across_rows(x)
    own_z = at[0] % Z
    block_a = join([up[2], up[1], shard, down[1], down[2]])
    low_a, high_a = along_y(block_a, 1), along_y(block_a, -1)
    up.append(along_z(up[2], 1))
    down.append(along_z(down[2], -1))
    up.append(along_z(after(up[3], block_a), 1))
    block_b = join([up[4], up[3], down[3]])
    x_up = after(jnp.where(own_z == Z - 1, crossed, x), up[4], down[3])
    x_down = after(jnp.where(own_z == 0, crossed, x), up[4], down[3])
    low1, high1 = along_z(x_up, 1), along_z(x_down, -1)
    low_b = along_y(block_b, 1)
    window, normed, w_kv_near = own_tile(after(x, block_b), modulation[0], w_kv[0], gains[1:2])
    high_b = along_y(after(block_b, normed, low_a, high_a), -1)
    low2, high2 = along_z(low1, 1, wrap=False), along_z(high1, -1, wrap=False)

    def add_tile(window, place, tile):
        return near_tile(place, scalars, tile, modulation[0], w_kv_near, gains[1:2], window)

    window = add_tile(add_tile(window, 0, low1), 1, high1)
    low_b, high_b, window = lax.optimization_barrier((low_b, high_b, window))
    edge = after(jnp.where(own_z == 0, high1, low1), low_b)
    edge_far = around_rows(edge)
    query_on, out_on_a, out_on_b = onward(at, [low_a, after(low_b, edge)], [high_a, high_b])
    query_far = along_y_by_place(query_on, [-1] * (Z // 2) + [1] * (Z // 2))
    out_far_a = along_y_by_place(out_on_a, [1] * (Z // 2) + [-1] * (Z // 2))
    out_far_b = along_y_by_place(
        out_on_b, [-1] + [1] * (Z // 2 - 1) + [-1] * (Z // 2 - 1) + [1]
    )
    window = add_tile(add_tile(window, 2, low2), 3, high2)
    near_blocks = [block_a, low_a, high_a, block_b, low_b, high_b]
    sides = [(dy, zs) for zs in (zs_a, zs_b) for dy in (0, Y - 1, 1)]
    query_plan = [(dy, zs, 0) for dy, zs in sides] + [(2, zs_a + zs_b, 0)]
    out_plan = [(dy, zs, len(zs) * size) for dy, zs in sides] + [(2, zs_a, 0), (2, zs_b, 0)]
    query_pieces = near_blocks + [query_far]
    out_pieces = near_blocks + [out_far_a, out_far_b]

    query = project_query(at, normed, gains[0:1], query_pieces, query_plan)
    query, window, edge_far = lax.optimization_barrier((query, window, edge_far))
    window = add_tile(window, None, edge_far)
    attended = attend(scalars, query, window)
    attended, *out_pieces[-2:] = lax.optimization_barrier((attended, *out_pieces[-2:]))
    out_whole = whole_out(at, out_pieces, out_plan, gains.shape[1])
    count = rows // 2
    parts = [
        to_next_section(project_out(attended, out_whole, gate, x, begin, count))
        for begin in (0, count)
    ]
    return jnp.concatenate(parts, axis=0)[None, None]


def solution(mesh):
    placed = (
        P("section", "patch", None, None),
        P("section", None, None),
        P("section", None),
        P("section", "patch", None),
        P("section", None, None),
        P("section", "patch", None),
        P("section", None, None),
        P("patch", None),
        P("patch"),
    )
    return jax.shard_map(
        on_device,
        mesh=mesh,
        in_specs=placed,
        out_specs=P("section", "patch", None, None),
        check_vma=False,
    )
```

```python
import math

import jax
import jax.numpy as jnp
from jax import lax
from jax.experimental import pallas as pl
from jax.experimental.pallas import tpu as pltpu
from jax.sharding import PartitionSpec as P

HEADS = 12
HEAD_DIM = 128
SPAN = 2
NB = 4
Y, Z = 4, 8
COLS = 512
SMALL = 12 * 1024 * 1024
LARGE = 20 * 1024 * 1024
VMEM = pl.BlockSpec(memory_space=pltpu.VMEM)
SMEM = pl.BlockSpec(memory_space=pltpu.SMEM)
HBM = pl.BlockSpec(memory_space=pltpu.HBM)
OFFSETS = [-1, 1, -2, 2]


def along_z(value, steps, wrap=True):
    pairs = [
        (y * Z + z, y * Z + (z + steps) % Z)
        for y in range(Y)
        for z in range(Z)
        if wrap or 0 <= z + steps < Z
    ]
    return lax.ppermute(value, "patch", pairs)


def around_rows(value):
    ends = [(y * Z + Z - 1, (y + 1) * Z) for y in range(Y - 1)]
    return lax.ppermute(value, "patch", ends + [(b, a) for a, b in ends])


def along_y(value, steps):
    return lax.ppermute(
        value, "patch", [(y * Z + z, ((y + steps) % Y) * Z + z) for y in range(Y) for z in range(Z)]
    )


def along_y_by_place(value, steps):
    pairs = [(y * Z + z, ((y + steps[z]) % Y) * Z + z) for y in range(Y) for z in range(Z)]
    return lax.ppermute(value, "patch", pairs)


def across_rows(value):
    pairs = [(y * Z + Z - 1, (y + 1) * Z + Z - 1) for y in range(Y - 1)]
    pairs += [((y + 1) * Z, y * Z) for y in range(Y - 1)]
    return lax.ppermute(value, "patch", pairs)


def to_next_section(block):
    count = lax.axis_size("section")
    return lax.ppermute(block, "section", [(i, (i + 1) % count) for i in range(count)])


def norm_rows(x, modulation):
    values = x.astype(jnp.float32)
    width = values.shape[1]
    average = jnp.sum(values, axis=-1, keepdims=True) * (1.0 / width)
    centered = values - average
    variance = jnp.sum(centered * centered, axis=-1, keepdims=True) * (1.0 / width)
    scaled = centered * lax.rsqrt(variance + 1e-06)
    return (scaled * (1.0 + modulation[1:2]) + modulation[0:1]).astype(jnp.bfloat16)


def head_norm(raw, gains):
    parts = []
    for h in range(raw.shape[1] // HEAD_DIM):
        piece = raw[:, h * HEAD_DIM : (h + 1) * HEAD_DIM]
        square = jnp.sum(piece * piece, axis=-1, keepdims=True) * (1.0 / HEAD_DIM)
        gain = gains[:, h * HEAD_DIM : (h + 1) * HEAD_DIM]
        parts.append((piece * lax.rsqrt(square + 1e-06) * gain).astype(jnp.bfloat16))
    return jnp.concatenate(parts, axis=1) if len(parts) > 1 else parts[0]


def kernel(body, name, specs, shapes, scratch, aliases, flops, limit, operands):
    moved = sum(o.size * o.dtype.itemsize for o in operands)
    return pl.pallas_call(
        body,
        in_specs=specs,
        out_specs=[VMEM for _ in shapes],
        out_shape=shapes,
        scratch_shapes=scratch,
        input_output_aliases=aliases,
        compiler_params=pltpu.CompilerParams(vmem_limit_bytes=limit),
        cost_estimate=pl.CostEstimate(flops=flops, transcendentals=0, bytes_accessed=moved),
        name=name,
    )(*operands)


def after(value, *others):
    return lax.optimization_barrier((value, *others))[0]


def own_tile(x, modulation, w_kv, gains):
    rows, width = x.shape
    wide = w_kv.shape[1]
    steps = wide // COLS

    def body(x_hbm, modulation_ref, w_hbm, gain_ref, window_ref, normed_ref, w_ref, x_ref, sems):
        def fetch(j):
            cols = pl.ds(pl.multiple_of(j * COLS, COLS), COLS)
            return pltpu.make_async_copy(w_hbm.at[:, cols], w_ref.at[:, cols], sems.at[j])

        rows_in = pltpu.make_async_copy(x_hbm, x_ref, sems.at[steps])
        rows_in.start()
        for j in range(steps):
            fetch(j).start()
        rows_in.wait()
        normed_ref[...] = norm_rows(x_ref[...], modulation_ref)

        @pl.loop(0, steps // 2)
        def _(j):
            fetch(j).wait()
            cols = pl.ds(pl.multiple_of(j * COLS, COLS), COLS)
            raw = jnp.dot(normed_ref[...], w_ref[:, cols], preferred_element_type=jnp.float32)
            window_ref[2 * SPAN, :, cols] = head_norm(raw, gain_ref[:, cols])

        @pl.loop(steps // 2, steps)
        def _(j):
            fetch(j).wait()
            cols = pl.ds(pl.multiple_of(j * COLS, COLS), COLS)
            raw = jnp.dot(normed_ref[...], w_ref[:, cols], preferred_element_type=jnp.float32)
            window_ref[2 * SPAN, :, cols] = raw.astype(jnp.bfloat16)

    shapes = [
        jax.ShapeDtypeStruct((2 * SPAN + 1, rows, wide), jnp.bfloat16),
        jax.ShapeDtypeStruct((rows, width), jnp.bfloat16),
        jax.ShapeDtypeStruct(w_kv.shape, w_kv.dtype),
    ]
    scratch = [pltpu.VMEM((rows, width), x.dtype), pltpu.SemaphoreType.DMA((steps + 1,))]
    flops = 2 * rows * width * wide
    x, w_kv = (pltpu.with_memory_space_constraint(o, pltpu.HBM) for o in (x, w_kv))
    operands = [x, modulation, w_kv, gains]
    specs = [HBM, VMEM, HBM, VMEM]
    return kernel(body, "own_tile", specs, shapes, scratch, {}, flops, SMALL, operands)


def near_tile(place, scalars, tile, modulation, w_kv, gains, window):
    rows, width = tile.shape
    wide = w_kv.shape[1]

    def body(
        at_ref, list_ref, live_ref, x_ref, modulation_ref, w_ref, gain_ref, _, window_ref, normed
    ):
        own_z = at_ref[0] % Z
        if place is None:
            spot = jnp.where(own_z == 0, 2, 3)
            offset = jnp.where(own_z == 0, OFFSETS[2], OFFSETS[3])
            here = (own_z == 0) | (own_z == Z - 1)
        else:
            spot, offset = place, OFFSETS[place]
            here = {0: True, 1: True, 2: own_z != 0, 3: own_z != Z - 1}[place]
        named = False
        for j in range(1, NB):
            named = named | ((list_ref[j] - at_ref[0] == offset) & (live_ref[0] > j))

        @pl.when(named & here)
        def _():
            normed[...] = norm_rows(x_ref[...], modulation_ref)

            @pl.loop(0, wide // (2 * COLS))
            def _(j):
                cols = pl.ds(pl.multiple_of(j * COLS, COLS), COLS)
                raw = jnp.dot(normed[...], w_ref[:, cols], preferred_element_type=jnp.float32)
                window_ref[spot, :, cols] = head_norm(raw, gain_ref[:, cols])
                cols = pl.ds(pl.multiple_of(wide // 2 + j * COLS, COLS), COLS)
                raw = jnp.dot(normed[...], w_ref[:, cols], preferred_element_type=jnp.float32)
                window_ref[spot, :, cols] = raw.astype(jnp.bfloat16)

    shapes = [jax.ShapeDtypeStruct(window.shape, window.dtype)]
    specs = [SMEM] * 3 + [VMEM] * 5
    scratch = [pltpu.VMEM((rows, width), jnp.bfloat16)]
    operands = [*scalars, tile, modulation, w_kv, gains, window]
    flops = 2 * rows * width * wide
    aliases = {len(operands) - 1: 0}
    return kernel(body, "near_tile", specs, shapes, scratch, aliases, flops, SMALL, operands)[0]


def join(parts):
    rows, width = parts[0].shape
    count = rows // 2

    def body(*refs):
        whole = refs[-1]
        second = count * len(parts)
        for k, ref in enumerate(refs[:-1]):
            whole[k * count : (k + 1) * count, :] = ref[:count, :]
            whole[second + k * count : second + (k + 1) * count, :] = ref[count:, :]

    shapes = [jax.ShapeDtypeStruct((len(parts) * rows, width), parts[0].dtype)]
    return kernel(body, "join", [VMEM] * len(parts), shapes, [], {}, 1, SMALL, parts)[0]


def onward(at, lows, highs):
    width = lows[0].shape[1]
    halves = [low.shape[0] // 2 for low in lows]
    begins = [sum(halves[:k]) for k in range(len(halves))]
    count = len(lows)

    def body(at_ref, *refs):
        low_refs, high_refs = refs[:count], refs[count : 2 * count]
        query_ref, out_refs = refs[2 * count], refs[2 * count + 1 :]
        own_z = at_ref[0] % Z
        left = own_z < Z // 2
        right = jnp.logical_not(left)
        end = (own_z == 0) | (own_z == Z - 1)
        for pick, source in ((left, high_refs), (right, low_refs)):

            @pl.when(pick)
            def _(source=source):
                for k, (begin, half) in enumerate(zip(begins, halves, strict=True)):
                    query_ref[begin : begin + half, :] = source[k][:half, :]

        for k, half in enumerate(halves):
            from_low = left if k < count - 1 else left != end
            for pick, source in ((from_low, low_refs), (jnp.logical_not(from_low), high_refs)):

                @pl.when(pick)
                def _(k=k, half=half, source=source):
                    out_refs[k][...] = source[k][half:, :]

    sizes = [sum(halves), *halves]
    shapes = [jax.ShapeDtypeStruct((n, width), lows[0].dtype) for n in sizes]
    specs = [SMEM] + [VMEM] * (2 * count)
    return kernel(body, "onward", specs, shapes, [], {}, 1, SMALL, [at, *lows, *highs])


def place_rows(at_ref, sources, plan, size, target):
    own_y, own_z = at_ref[0] // Z, at_ref[0] % Z
    for ref, (dy, zs, begin) in zip(sources, plan, strict=True):
        at_y = (own_y + dy) % Y
        for k, dz in enumerate(zs):
            shard = at_y * Z + (own_z + dz) % Z
            row = pl.multiple_of(shard * size, 16)
            target[pl.ds(row, size), :] = ref[begin + k * size : begin + (k + 1) * size, :]


def project_query(at, normed, gains, pieces, plan):
    rows, width = normed.shape
    inner = gains.shape[1]
    size = width // (Y * Z)

    def body(at_ref, normed_ref, gain_ref, *refs):
        sources, (out_ref, whole) = refs[: len(pieces)], refs[len(pieces) :]
        place_rows(at_ref, sources, plan, size, whole)
        for j in range(inner // COLS):
            cols = slice(j * COLS, (j + 1) * COLS)
            raw = jnp.dot(normed_ref[...], whole[:, cols], preferred_element_type=jnp.float32)
            out_ref[:, cols] = head_norm(raw, gain_ref[:, cols])

    shapes = [jax.ShapeDtypeStruct((rows, inner), jnp.bfloat16)]
    scratch = [pltpu.VMEM((width, inner), jnp.bfloat16)]
    specs = [SMEM] + [VMEM] * (2 + len(pieces))
    operands = [at, normed, gains, *pieces]
    flops = 2 * rows * width * inner
    return kernel(body, "project_query", specs, shapes, scratch, {}, flops, SMALL, operands)[0]


def whole_out(at, pieces, plan, inner):
    width = pieces[0].shape[1]
    size = inner // (Y * Z)

    def body(at_ref, *refs):
        place_rows(at_ref, refs[: len(pieces)], plan, size, refs[-1])

    shapes = [jax.ShapeDtypeStruct((inner, width), jnp.bfloat16)]
    specs = [SMEM] + [VMEM] * len(pieces)
    return kernel(body, "whole_out", specs, shapes, [], {}, 1, SMALL, [at, *pieces])[0]


def attend(scalars, query, window, at, rows):
    inner = query.shape[1]
    factor = math.log2(math.e) / math.sqrt(HEAD_DIM)

    def body(at_ref, list_ref, live_ref, q_ref, window_ref, out_ref):
        def place(j):
            away = list_ref[j] - at_ref[0]
            found = jnp.where(away < 0, -2 * away - 2, 2 * away - 1)
            return jnp.where(away == 0, 2 * SPAN, jnp.clip(found, 0, 2 * SPAN - 1))

        def head(h, places):
            begin = pl.multiple_of(h * HEAD_DIM, HEAD_DIM)
            cols = pl.ds(begin, HEAD_DIM)
            value_cols = pl.ds(begin + inner, HEAD_DIM)
            q = q_ref[at : at + rows, cols]
            scores = []
            for p in places:
                keys = window_ref[p, :, cols]
                scores.append(
                    lax.dot_general(
                        q, keys, (((1,), (1,)), ((), ())), preferred_element_type=jnp.float32
                    )
                )
            highest = jnp.max(scores[0], axis=-1, keepdims=True)
            for s in scores[1:]:
                highest = jnp.maximum(highest, jnp.max(s, axis=-1, keepdims=True))
            total = mixed = None
            for s, p in zip(scores, places, strict=True):
                weight = jnp.exp2((s - highest) * factor)
                line = jnp.sum(weight, axis=-1, keepdims=True)
                term = jnp.dot(
                    weight.astype(jnp.bfloat16),
                    window_ref[p, :, value_cols],
                    preferred_element_type=jnp.float32,
                )
                total = line if total is None else total + line
                mixed = term if mixed is None else mixed + term
            out_ref[:, cols] = (mixed * (1.0 / total)).astype(jnp.bfloat16)

        for live in range(2, NB + 1):

            @pl.when(live_ref[0] == live)
            def _(live=live):
                places = [2 * SPAN] + [place(j) for j in range(1, live)]

                @pl.loop(0, HEADS // 2)
                def _(pair):
                    head(2 * pair, places)
                    head(2 * pair + 1, places)

    shapes = [jax.ShapeDtypeStruct((rows, inner), jnp.bfloat16)]
    flops = 4 * rows * NB * window.shape[1] * inner
    operands = [*scalars, query, window]
    specs = [SMEM] * 3 + [VMEM] * 2
    return kernel(body, "attend", specs, shapes, [], {}, flops, LARGE, operands)[0]


def project_out(attended, w_out, gate, x, at):
    count = attended.shape[0]
    width = w_out.shape[1]

    def body(a_ref, w_ref, gate_ref, x_ref, out_ref):
        for j in range(width // COLS):
            cols = slice(j * COLS, (j + 1) * COLS)
            branch = jnp.dot(a_ref[...], w_ref[:, cols], preferred_element_type=jnp.float32)
            residual = x_ref[at : at + count, cols].astype(jnp.float32)
            out_ref[:, cols] = (residual + gate_ref[:, cols] * branch).astype(jnp.bfloat16)

    shapes = [jax.ShapeDtypeStruct((count, width), jnp.bfloat16)]
    flops = 2 * count * width * w_out.shape[0]
    operands = [attended, w_out, gate, x]
    return kernel(body, "project_out", [VMEM] * 4, shapes, [], {}, flops, SMALL, operands)[0]


def on_device(arriving, modulation, gate, w_query, w_kv, w_out, qk_gain, neighbors, live):
    x = arriving[0, 0]
    rows = x.shape[0]
    at = lax.axis_index("patch").astype(jnp.int32).reshape(1)
    size = w_query.shape[1]
    scalars = [at, neighbors[0], live]
    gains = qk_gain[0]

    shard = jnp.concatenate([w_query[0], w_out[0]], axis=0)
    zs_a, zs_b = [-2, -1, 0, 1, 2], [-4, -3, 3]
    up, down = [shard], [shard]
    for k in range(1, 3):
        up.append(along_z(up[-1], 1))
        down.append(along_z(down[-1], -1))
    crossed = across_rows(x)
    own_z = at[0] % Z
    block_a = join([up[2], up[1], shard, down[1], down[2]])
    low_a, high_a = along_y(block_a, 1), along_y(block_a, -1)
    up.append(along_z(up[2], 1))
    down.append(along_z(down[2], -1))
    up.append(along_z(after(up[3], block_a), 1))
    block_b = join([up[4], up[3], down[3]])
    x_up = after(jnp.where(own_z == Z - 1, crossed, x), up[4], down[3])
    x_down = after(jnp.where(own_z == 0, crossed, x), up[4], down[3])
    low1, high1 = along_z(x_up, 1), along_z(x_down, -1)
    low_b = along_y(block_b, 1)
    window, normed, w_kv_near = own_tile(after(x, block_b), modulation[0], w_kv[0], gains[1:2])
    high_b = along_y(after(block_b, normed, low_a, high_a), -1)
    low2, high2 = along_z(low1, 1, wrap=False), along_z(high1, -1, wrap=False)

    def add_tile(window, place, tile):
        return near_tile(place, scalars, tile, modulation[0], w_kv_near, gains[1:2], window)

    window = add_tile(add_tile(window, 0, low1), 1, high1)
    low_b, high_b, window = lax.optimization_barrier((low_b, high_b, window))
    edge = after(jnp.where(own_z == 0, high1, low1), low_b)
    edge_far = around_rows(edge)
    query_on, out_on_a, out_on_b = onward(at, [low_a, after(low_b, edge)], [high_a, high_b])
    query_far = along_y_by_place(query_on, [-1] * (Z // 2) + [1] * (Z // 2))
    out_far_a = along_y_by_place(out_on_a, [1] * (Z // 2) + [-1] * (Z // 2))
    out_far_b = along_y_by_place(
        out_on_b, [-1] + [1] * (Z // 2 - 1) + [-1] * (Z // 2 - 1) + [1]
    )
    window = add_tile(add_tile(window, 2, low2), 3, high2)
    near_blocks = [block_a, low_a, high_a, block_b, low_b, high_b]
    sides = [(dy, zs) for zs in (zs_a, zs_b) for dy in (0, Y - 1, 1)]
    query_plan = [(dy, zs, 0) for dy, zs in sides] + [(2, zs_a + zs_b, 0)]
    out_plan = [(dy, zs, len(zs) * size) for dy, zs in sides] + [(2, zs_a, 0), (2, zs_b, 0)]
    query_pieces = near_blocks + [query_far]
    out_pieces = near_blocks + [out_far_a, out_far_b]

    query = project_query(at, normed, gains[0:1], query_pieces, query_plan)
    query, window, edge_far = lax.optimization_barrier((query, window, edge_far))
    window = add_tile(window, None, edge_far)
    count = rows // 2
    attended = attend(scalars, query, window, 0, count)
    attended, *out_pieces[-2:] = lax.optimization_barrier((attended, *out_pieces[-2:]))
    out_whole = whole_out(at, out_pieces, out_plan, gains.shape[1])
    first = project_out(attended, out_whole, gate, x, 0)
    first_handed = to_next_section(first)
    attended = attend(scalars, after(query, first), window, count, count)
    second = project_out(attended, out_whole, gate, x, count)
    parts = [first_handed, to_next_section(after(second, first_handed))]
    return jnp.concatenate(parts, axis=0)[None, None]


def solution(mesh):
    placed = (
        P("section", "patch", None, None),
        P("section", None, None),
        P("section", None),
        P("section", "patch", None),
        P("section", None, None),
        P("section", "patch", None),
        P("section", None, None),
        P("patch", None),
        P("patch"),
    )
    return jax.shard_map(
        on_device,
        mesh=mesh,
        in_specs=placed,
        out_specs=P("section", "patch", None, None),
        check_vma=False,
    )
```

```python
import math

import jax
import jax.numpy as jnp
from jax import lax
from jax.experimental import pallas as pl
from jax.experimental.pallas import tpu as pltpu
from jax.sharding import PartitionSpec as P

HEADS = 12
HEAD_DIM = 128
SPAN = 2
NB = 4
Y, Z = 4, 8
COLS = 512
SMALL = 12 * 1024 * 1024
LARGE = 20 * 1024 * 1024
VMEM = pl.BlockSpec(memory_space=pltpu.VMEM)
SMEM = pl.BlockSpec(memory_space=pltpu.SMEM)
HBM = pl.BlockSpec(memory_space=pltpu.HBM)
OFFSETS = [-1, 1, -2, 2]


def along_z(value, steps, wrap=True):
    pairs = [
        (y * Z + z, y * Z + (z + steps) % Z)
        for y in range(Y)
        for z in range(Z)
        if wrap or 0 <= z + steps < Z
    ]
    return lax.ppermute(value, "patch", pairs)


def around_rows(value):
    ends = [(y * Z + Z - 1, (y + 1) * Z) for y in range(Y - 1)]
    return lax.ppermute(value, "patch", ends + [(b, a) for a, b in ends])


def along_y(value, steps):
    return lax.ppermute(
        value, "patch", [(y * Z + z, ((y + steps) % Y) * Z + z) for y in range(Y) for z in range(Z)]
    )


def along_y_by_place(value, steps):
    pairs = [(y * Z + z, ((y + steps[z]) % Y) * Z + z) for y in range(Y) for z in range(Z)]
    return lax.ppermute(value, "patch", pairs)


def across_rows(value):
    pairs = [(y * Z + Z - 1, (y + 1) * Z + Z - 1) for y in range(Y - 1)]
    pairs += [((y + 1) * Z, y * Z) for y in range(Y - 1)]
    return lax.ppermute(value, "patch", pairs)


def to_next_section(block):
    count = lax.axis_size("section")
    return lax.ppermute(block, "section", [(i, (i + 1) % count) for i in range(count)])


def norm_rows(x, modulation):
    values = x.astype(jnp.float32)
    width = values.shape[1]
    average = jnp.sum(values, axis=-1, keepdims=True) * (1.0 / width)
    centered = values - average
    variance = jnp.sum(centered * centered, axis=-1, keepdims=True) * (1.0 / width)
    scaled = centered * lax.rsqrt(variance + 1e-06)
    return (scaled * (1.0 + modulation[1:2]) + modulation[0:1]).astype(jnp.bfloat16)


def head_norm(raw, gains):
    parts = []
    for h in range(raw.shape[1] // HEAD_DIM):
        piece = raw[:, h * HEAD_DIM : (h + 1) * HEAD_DIM]
        square = jnp.sum(piece * piece, axis=-1, keepdims=True) * (1.0 / HEAD_DIM)
        gain = gains[:, h * HEAD_DIM : (h + 1) * HEAD_DIM]
        parts.append((piece * lax.rsqrt(square + 1e-06) * gain).astype(jnp.bfloat16))
    return jnp.concatenate(parts, axis=1) if len(parts) > 1 else parts[0]


def kernel(body, name, specs, shapes, scratch, aliases, flops, limit, operands):
    moved = sum(o.size * o.dtype.itemsize for o in operands)
    return pl.pallas_call(
        body,
        in_specs=specs,
        out_specs=[VMEM for _ in shapes],
        out_shape=shapes,
        scratch_shapes=scratch,
        input_output_aliases=aliases,
        compiler_params=pltpu.CompilerParams(vmem_limit_bytes=limit),
        cost_estimate=pl.CostEstimate(flops=flops, transcendentals=0, bytes_accessed=moved),
        name=name,
    )(*operands)


def after(value, *others):
    return lax.optimization_barrier((value, *others))[0]


def own_tile(x, modulation, w_kv, gains):
    rows, width = x.shape
    wide = w_kv.shape[1]
    steps = wide // COLS

    def body(x_hbm, modulation_ref, w_hbm, gain_ref, window_ref, normed_ref, w_ref, x_ref, sems):
        def fetch(j):
            cols = pl.ds(pl.multiple_of(j * COLS, COLS), COLS)
            return pltpu.make_async_copy(w_hbm.at[:, cols], w_ref.at[:, cols], sems.at[j])

        rows_in = pltpu.make_async_copy(x_hbm, x_ref, sems.at[steps])
        rows_in.start()
        for j in range(steps):
            fetch(j).start()
        rows_in.wait()
        normed_ref[...] = norm_rows(x_ref[...], modulation_ref)

        @pl.loop(0, steps // 2)
        def _(j):
            fetch(j).wait()
            cols = pl.ds(pl.multiple_of(j * COLS, COLS), COLS)
            raw = jnp.dot(normed_ref[...], w_ref[:, cols], preferred_element_type=jnp.float32)
            window_ref[2 * SPAN, :, cols] = head_norm(raw, gain_ref[:, cols])

        @pl.loop(steps // 2, steps)
        def _(j):
            fetch(j).wait()
            cols = pl.ds(pl.multiple_of(j * COLS, COLS), COLS)
            raw = jnp.dot(normed_ref[...], w_ref[:, cols], preferred_element_type=jnp.float32)
            window_ref[2 * SPAN, :, cols] = raw.astype(jnp.bfloat16)

    shapes = [
        jax.ShapeDtypeStruct((2 * SPAN + 1, rows, wide), jnp.bfloat16),
        jax.ShapeDtypeStruct((rows, width), jnp.bfloat16),
        jax.ShapeDtypeStruct(w_kv.shape, w_kv.dtype),
    ]
    scratch = [pltpu.VMEM((rows, width), x.dtype), pltpu.SemaphoreType.DMA((steps + 1,))]
    flops = 2 * rows * width * wide
    x, w_kv = (pltpu.with_memory_space_constraint(o, pltpu.HBM) for o in (x, w_kv))
    operands = [x, modulation, w_kv, gains]
    specs = [HBM, VMEM, HBM, VMEM]
    return kernel(body, "own_tile", specs, shapes, scratch, {}, flops, SMALL, operands)


def near_tile(place, scalars, tile, modulation, w_kv, gains, window):
    rows, width = tile.shape
    wide = w_kv.shape[1]

    def body(
        at_ref, list_ref, live_ref, x_ref, modulation_ref, w_ref, gain_ref, _, window_ref, normed
    ):
        own_z = at_ref[0] % Z
        if place is None:
            spot = jnp.where(own_z == 0, 2, 3)
            offset = jnp.where(own_z == 0, OFFSETS[2], OFFSETS[3])
            here = (own_z == 0) | (own_z == Z - 1)
        else:
            spot, offset = place, OFFSETS[place]
            here = {0: True, 1: True, 2: own_z != 0, 3: own_z != Z - 1}[place]
        named = False
        for j in range(1, NB):
            named = named | ((list_ref[j] - at_ref[0] == offset) & (live_ref[0] > j))

        @pl.when(named & here)
        def _():
            normed[...] = norm_rows(x_ref[...], modulation_ref)

            @pl.loop(0, wide // (2 * COLS))
            def _(j):
                cols = pl.ds(pl.multiple_of(j * COLS, COLS), COLS)
                raw = jnp.dot(normed[...], w_ref[:, cols], preferred_element_type=jnp.float32)
                window_ref[spot, :, cols] = head_norm(raw, gain_ref[:, cols])
                cols = pl.ds(pl.multiple_of(wide // 2 + j * COLS, COLS), COLS)
                raw = jnp.dot(normed[...], w_ref[:, cols], preferred_element_type=jnp.float32)
                window_ref[spot, :, cols] = raw.astype(jnp.bfloat16)

    shapes = [jax.ShapeDtypeStruct(window.shape, window.dtype)]
    specs = [SMEM] * 3 + [VMEM] * 5
    scratch = [pltpu.VMEM((rows, width), jnp.bfloat16)]
    operands = [*scalars, tile, modulation, w_kv, gains, window]
    flops = 2 * rows * width * wide
    aliases = {len(operands) - 1: 0}
    return kernel(body, "near_tile", specs, shapes, scratch, aliases, flops, SMALL, operands)[0]


def join(parts):
    rows, width = parts[0].shape
    count = rows // 2

    def body(*refs):
        whole = refs[-1]
        second = count * len(parts)
        for k, ref in enumerate(refs[:-1]):
            whole[k * count : (k + 1) * count, :] = ref[:count, :]
            whole[second + k * count : second + (k + 1) * count, :] = ref[count:, :]

    shapes = [jax.ShapeDtypeStruct((len(parts) * rows, width), parts[0].dtype)]
    return kernel(body, "join", [VMEM] * len(parts), shapes, [], {}, 1, SMALL, parts)[0]


def onward(at, lows, highs):
    width = lows[0].shape[1]
    halves = [low.shape[0] // 2 for low in lows]
    begins = [sum(halves[:k]) for k in range(len(halves))]
    count = len(lows)

    def body(at_ref, *refs):
        low_refs, high_refs = refs[:count], refs[count : 2 * count]
        query_ref, out_refs = refs[2 * count], refs[2 * count + 1 :]
        own_z = at_ref[0] % Z
        left = own_z < Z // 2
        right = jnp.logical_not(left)
        end = (own_z == 0) | (own_z == Z - 1)
        for pick, source in ((left, high_refs), (right, low_refs)):

            @pl.when(pick)
            def _(source=source):
                for k, (begin, half) in enumerate(zip(begins, halves, strict=True)):
                    query_ref[begin : begin + half, :] = source[k][:half, :]

        for k, half in enumerate(halves):
            from_low = left if k < count - 1 else left != end
            for pick, source in ((from_low, low_refs), (jnp.logical_not(from_low), high_refs)):

                @pl.when(pick)
                def _(k=k, half=half, source=source):
                    out_refs[k][...] = source[k][half:, :]

    sizes = [sum(halves), *halves]
    shapes = [jax.ShapeDtypeStruct((n, width), lows[0].dtype) for n in sizes]
    specs = [SMEM] + [VMEM] * (2 * count)
    return kernel(body, "onward", specs, shapes, [], {}, 1, SMALL, [at, *lows, *highs])


def place_rows(at_ref, sources, plan, size, target):
    own_y, own_z = at_ref[0] // Z, at_ref[0] % Z
    for ref, (dy, zs, begin) in zip(sources, plan, strict=True):
        at_y = (own_y + dy) % Y
        for k, dz in enumerate(zs):
            shard = at_y * Z + (own_z + dz) % Z
            row = pl.multiple_of(shard * size, 16)
            target[pl.ds(row, size), :] = ref[begin + k * size : begin + (k + 1) * size, :]


def project_query(at, normed, gains, pieces, plan):
    rows, width = normed.shape
    inner = gains.shape[1]
    size = width // (Y * Z)

    def body(at_ref, normed_ref, gain_ref, *refs):
        sources, (out_ref, whole) = refs[: len(pieces)], refs[len(pieces) :]
        place_rows(at_ref, sources, plan, size, whole)
        for j in range(inner // COLS):
            cols = slice(j * COLS, (j + 1) * COLS)
            raw = jnp.dot(normed_ref[...], whole[:, cols], preferred_element_type=jnp.float32)
            out_ref[:, cols] = head_norm(raw, gain_ref[:, cols])

    shapes = [jax.ShapeDtypeStruct((rows, inner), jnp.bfloat16)]
    scratch = [pltpu.VMEM((width, inner), jnp.bfloat16)]
    specs = [SMEM] + [VMEM] * (2 + len(pieces))
    operands = [at, normed, gains, *pieces]
    flops = 2 * rows * width * inner
    return kernel(body, "project_query", specs, shapes, scratch, {}, flops, SMALL, operands)[0]


def whole_out(at, pieces, plan, inner):
    width = pieces[0].shape[1]
    size = inner // (Y * Z)

    def body(at_ref, *refs):
        place_rows(at_ref, refs[: len(pieces)], plan, size, refs[-1])

    shapes = [jax.ShapeDtypeStruct((inner, width), jnp.bfloat16)]
    specs = [SMEM] + [VMEM] * len(pieces)
    return kernel(body, "whole_out", specs, shapes, [], {}, 1, SMALL, [at, *pieces])[0]


def attend(scalars, query, window, at, rows):
    inner = query.shape[1]
    factor = math.log2(math.e) / math.sqrt(HEAD_DIM)

    def body(at_ref, list_ref, live_ref, q_ref, window_ref, out_ref):
        def place(j):
            away = list_ref[j] - at_ref[0]
            found = jnp.where(away < 0, -2 * away - 2, 2 * away - 1)
            return jnp.where(away == 0, 2 * SPAN, jnp.clip(found, 0, 2 * SPAN - 1))

        def head(h, places):
            begin = pl.multiple_of(h * HEAD_DIM, HEAD_DIM)
            cols = pl.ds(begin, HEAD_DIM)
            value_cols = pl.ds(begin + inner, HEAD_DIM)
            q = q_ref[at : at + rows, cols]
            scores = []
            for p in places:
                keys = window_ref[p, :, cols]
                scores.append(
                    lax.dot_general(
                        q, keys, (((1,), (1,)), ((), ())), preferred_element_type=jnp.float32
                    )
                )
            highest = jnp.max(scores[0], axis=-1, keepdims=True)
            for s in scores[1:]:
                highest = jnp.maximum(highest, jnp.max(s, axis=-1, keepdims=True))
            total = mixed = None
            for s, p in zip(scores, places, strict=True):
                weight = jnp.exp2((s - highest) * factor)
                line = jnp.sum(weight, axis=-1, keepdims=True)
                term = jnp.dot(
                    weight.astype(jnp.bfloat16),
                    window_ref[p, :, value_cols],
                    preferred_element_type=jnp.float32,
                )
                total = line if total is None else total + line
                mixed = term if mixed is None else mixed + term
            out_ref[:, cols] = (mixed * (1.0 / total)).astype(jnp.bfloat16)

        for live in range(2, NB + 1):

            @pl.when(live_ref[0] == live)
            def _(live=live):
                places = [2 * SPAN] + [place(j) for j in range(1, live)]

                @pl.loop(0, HEADS // 2)
                def _(pair):
                    head(2 * pair, places)
                    head(2 * pair + 1, places)

    shapes = [jax.ShapeDtypeStruct((rows, inner), jnp.bfloat16)]
    flops = 4 * rows * NB * window.shape[1] * inner
    operands = [*scalars, query, window]
    specs = [SMEM] * 3 + [VMEM] * 2
    return kernel(body, "attend", specs, shapes, [], {}, flops, LARGE, operands)[0]


def project_out(attended, w_out, gate, x, at):
    count = attended.shape[0]
    width = w_out.shape[1]

    def body(a_ref, w_ref, gate_ref, x_hbm, out_ref, x_ref, sem):
        rows_in = pltpu.make_async_copy(x_hbm.at[at : at + count, :], x_ref, sem)
        rows_in.start()
        for j in range(width // COLS):
            cols = slice(j * COLS, (j + 1) * COLS)
            branch = jnp.dot(a_ref[...], w_ref[:, cols], preferred_element_type=jnp.float32)
            if j == 0:
                rows_in.wait()
            residual = x_ref[:, cols].astype(jnp.float32)
            out_ref[:, cols] = (residual + gate_ref[:, cols] * branch).astype(jnp.bfloat16)

    x = pltpu.with_memory_space_constraint(x, pltpu.HBM)
    shapes = [jax.ShapeDtypeStruct((count, width), jnp.bfloat16)]
    scratch = [pltpu.VMEM((count, width), x.dtype), pltpu.SemaphoreType.DMA(())]
    flops = 2 * count * width * w_out.shape[0]
    operands = [attended, w_out, gate, x]
    specs = [VMEM] * 3 + [HBM]
    return kernel(body, "project_out", specs, shapes, scratch, {}, flops, SMALL, operands)[0]


def on_device(arriving, modulation, gate, w_query, w_kv, w_out, qk_gain, neighbors, live):
    x = arriving[0, 0]
    rows = x.shape[0]
    at = lax.axis_index("patch").astype(jnp.int32).reshape(1)
    size = w_query.shape[1]
    scalars = [at, neighbors[0], live]
    gains = qk_gain[0]

    shard = jnp.concatenate([w_query[0], w_out[0]], axis=0)
    zs_a, zs_b = [-2, -1, 0, 1, 2], [-4, -3, 3]
    up, down = [shard], [shard]
    for k in range(1, 3):
        up.append(along_z(up[-1], 1))
        down.append(along_z(down[-1], -1))
    crossed = across_rows(x)
    own_z = at[0] % Z
    block_a = join([up[2], up[1], shard, down[1], down[2]])
    low_a, high_a = along_y(block_a, 1), along_y(block_a, -1)
    up.append(along_z(up[2], 1))
    down.append(along_z(down[2], -1))
    up.append(along_z(after(up[3], block_a), 1))
    block_b = join([up[4], up[3], down[3]])
    x_up = after(jnp.where(own_z == Z - 1, crossed, x), up[4], down[3])
    x_down = after(jnp.where(own_z == 0, crossed, x), up[4], down[3])
    low1, high1 = along_z(x_up, 1), along_z(x_down, -1)
    low_b = along_y(block_b, 1)
    window, normed, w_kv_near = own_tile(after(x, block_b), modulation[0], w_kv[0], gains[1:2])
    high_b = along_y(after(block_b, normed, low_a, high_a), -1)
    low2, high2 = along_z(low1, 1, wrap=False), along_z(high1, -1, wrap=False)

    def add_tile(window, place, tile):
        return near_tile(place, scalars, tile, modulation[0], w_kv_near, gains[1:2], window)

    window = add_tile(add_tile(window, 0, low1), 1, high1)
    low_b, high_b, window = lax.optimization_barrier((low_b, high_b, window))
    edge = after(jnp.where(own_z == 0, high1, low1), low_b)
    edge_far = around_rows(edge)
    query_on, out_on_a, out_on_b = onward(at, [low_a, after(low_b, edge)], [high_a, high_b])
    query_far = along_y_by_place(query_on, [-1] * (Z // 2) + [1] * (Z // 2))
    out_far_a = along_y_by_place(out_on_a, [1] * (Z // 2) + [-1] * (Z // 2))
    out_far_b = along_y_by_place(
        out_on_b, [-1] + [1] * (Z // 2 - 1) + [-1] * (Z // 2 - 1) + [1]
    )
    window = add_tile(add_tile(window, 2, low2), 3, high2)
    near_blocks = [block_a, low_a, high_a, block_b, low_b, high_b]
    sides = [(dy, zs) for zs in (zs_a, zs_b) for dy in (0, Y - 1, 1)]
    query_plan = [(dy, zs, 0) for dy, zs in sides] + [(2, zs_a + zs_b, 0)]
    out_plan = [(dy, zs, len(zs) * size) for dy, zs in sides] + [(2, zs_a, 0), (2, zs_b, 0)]
    query_pieces = near_blocks + [query_far]
    out_pieces = near_blocks + [out_far_a, out_far_b]

    query = project_query(at, normed, gains[0:1], query_pieces, query_plan)
    query, window, edge_far = lax.optimization_barrier((query, window, edge_far))
    window = add_tile(window, None, edge_far)
    count = rows // 2
    attended = attend(scalars, query, window, 0, count)
    attended, *out_pieces[-2:] = lax.optimization_barrier((attended, *out_pieces[-2:]))
    out_whole = whole_out(at, out_pieces, out_plan, gains.shape[1])
    first = project_out(attended, out_whole, gate, x, 0)
    first_handed = to_next_section(first)
    attended = attend(scalars, after(query, first), window, count, count)
    second = project_out(attended, out_whole, gate, x, count)
    second_handed = to_next_section(after(second, first_handed))
    whole = lax.optimization_barrier(jnp.pad(first_handed, ((0, count), (0, 0))))
    return lax.dynamic_update_slice(whole, second_handed, (count, 0))[None, None]


def solution(mesh):
    placed = (
        P("section", "patch", None, None),
        P("section", None, None),
        P("section", None),
        P("section", "patch", None),
        P("section", None, None),
        P("section", "patch", None),
        P("section", None, None),
        P("patch", None),
        P("patch"),
    )
    return jax.shard_map(
        on_device,
        mesh=mesh,
        in_specs=placed,
        out_specs=P("section", "patch", None, None),
        check_vma=False,
    )
```
